256 devices in a mesh: outer: 16 (over y, x), inner: 16 (over z, core).
Axes of the slice: x: 4, y: 4, z: 8, core: 2. Of those that a mesh axis runs over, the one named last changes fastest.
Arguments:
- tokens: bfloat16 [65536, 8192], P(('outer', 'inner')), may hold values from -24 to 24
- upstream: bfloat16 [65536, 8192], P(('outer', 'inner')), may hold values from -24 to 24
- weights: bfloat16 [3, 8192, 256], P(None, ('outer', 'inner')), may hold values from -0.0625 to 0.0625
Outputs:
- gradients: float32 [3, 256, 8192], P(None, 'inner', 'outer')
The draws below stay inside these ranges and needn't reach their ends.
All inputs are finite; a program needn't handle non-finite values.
Results may differ from the reference program's by a relative error of at most 0.0049.
Values may be sent and summed in bfloat16 or wider, within the bound.
A program may use at most 128 MiB of HBM per device.

```python
import jax
import jax.numpy as jnp
from jax import lax

D = 8192
FFB = 256
TOK_DEV = 256
TOKENS = 65536
N_OUTER = 16
N_INNER = 16


def with_spikes(values, own_key, source, target, shards_of, factor):
    def block_of(position):
        return (jnp.arange(values.shape[position]) // (values.shape[position] // shards_of)).reshape((-1,) + (1,) * (values.ndim - 1 - position))

    one_side = jax.random.permutation(own_key, shards_of)[block_of(target)]
    other_side = (block_of(target) + shards_of // 2) % shards_of
    return jnp.where((block_of(source) == one_side) | (block_of(source) == other_side), factor * values, values)


def shard_levels(stream_key, extent, pieces, low, top_value):
    def one(position, parts):
        steps = jax.random.uniform(jax.random.fold_in(jax.random.fold_in(stream_key, 6), position), (parts,), jnp.float32, low / len(pieces), top_value / len(pieces))
        return jnp.repeat(jnp.exp(steps), extent[position] // parts).reshape((-1,) + (1,) * (len(extent) - position - 1))

    gain = one(*pieces[0])
    for cut in pieces[1:]:
        gain = gain * one(*cut)
    return gain


def bell_draw(stream_key, dims, width, limit, split=(), kind=jnp.bfloat16):
    drawn = width * jax.random.normal(stream_key, dims, jnp.float32)
    if split:
        drawn = drawn * shard_levels(stream_key, dims, split, -0.22, 0.18)
    return jnp.clip(drawn, -limit, limit).astype(kind)


def noise_with(stream_key, dims, scale, reach, split, heavy, dtype=jnp.bfloat16):
    values = scale * jax.random.normal(stream_key, dims, jnp.float32)
    if split:
        values = values * shard_levels(stream_key, dims, split, -0.22, 0.18)
    return jnp.clip(with_spikes(values, jax.random.fold_in(stream_key, 3), *heavy), -reach, reach).astype(dtype)


def setup_inputs(seed: int = 0) -> dict:
    streams_of = jax.random.split(jax.random.key(seed), 4)
    tokens = noise_with(streams_of[0], (TOKENS, D), 1.0, 24.0, ((0, 256),), (0, 1, 256, 6.0))
    upstream = noise_with(streams_of[1], (TOKENS, D), 1.0, 24.0, ((0, 256),), (0, 1, 256, 6.0))
    weights = bell_draw(streams_of[2], (3, D, FFB), D ** -0.5, 0.0625, ((1, 256),))
    return {"tokens": tokens, "upstream": upstream, "weights": weights}


def widen(values):
    return lax.optimization_barrier(values.astype(jnp.bfloat16)).astype(jnp.float32)


def block_terms(block_x, block_y, weights):
    gate_pre = jnp.dot(block_x, weights[0], preferred_element_type=jnp.float32)
    up_pre = jnp.dot(block_x, weights[1], preferred_element_type=jnp.float32)
    hidden_grad = jnp.dot(block_y, weights[2], preferred_element_type=jnp.float32)
    sigmoid = jax.nn.sigmoid(gate_pre)
    activated = gate_pre * sigmoid
    hidden = (activated * up_pre).astype(jnp.bfloat16)
    grad_gate = (hidden_grad * up_pre * sigmoid * (1.0 + gate_pre * (1.0 - sigmoid))).astype(jnp.bfloat16)
    grad_up = (hidden_grad * activated).astype(jnp.bfloat16)
    return jnp.stack([
        jnp.dot(grad_gate.T, block_x, preferred_element_type=jnp.float32),
        jnp.dot(grad_up.T, block_x, preferred_element_type=jnp.float32),
        jnp.dot(hidden.T, block_y, preferred_element_type=jnp.float32),
    ])


def reference(tokens, upstream, weights):
    token_blocks = tokens.reshape(N_OUTER, N_INNER, TOK_DEV, D)
    upstream_blocks = upstream.reshape(N_OUTER, N_INNER, TOK_DEV, D)
    zeros_block = jnp.zeros((3, FFB, D), jnp.float32)

    def inner_step(partial_sum, blocks):
        return partial_sum + widen(block_terms(blocks[0], blocks[1], weights)), None

    def outer_step(total, blocks):
        partial_sum, unused = lax.scan(inner_step, zeros_block, blocks)
        return total + widen(partial_sum), None

    total, unused = lax.scan(outer_step, zeros_block, (token_blocks, upstream_blocks))
    return total
```

```python
import jax
import jax.numpy as jnp
from jax import lax
from jax.experimental import pallas as pl
from jax.experimental.pallas import tpu as pltpu
from jax.sharding import PartitionSpec as P

MESH = pl.DeviceIdType.MESH
BF16, F32 = jnp.bfloat16, jnp.float32
NX, NY, NZ = 4, 4, 8
COLS = 512
HALF = COLS // 2
UNITS = 128
TOK = 256
MODEL = 8192


def place(x, y, z, c):
    return (y * NX + x, z * 2 + c)


class Links:
    def __init__(self, send_sems, recv_sems):
        self.send_sems, self.recv_sems = send_sems, recv_sems
        self.count = 0
        self.started = []

    def send(self, src, dst, target):
        k = self.count
        self.count += 1
        copy = pltpu.make_async_remote_copy(
            src_ref=src,
            dst_ref=dst,
            send_sem=self.send_sems.at[k],
            recv_sem=self.recv_sems.at[k],
            device_id=target,
            device_id_type=MESH,
        )
        copy.start()
        self.started.append(copy)
        return copy

    def drain(self):
        for copy in self.started:
            copy.wait_send()


N_COPIES = 256


def kernel(
    tokens,
    upstream,
    shard,
    out,
    tok,
    ups,
    full,
    stage,
    grads,
    down,
    sent1,
    got1,
    part1,
    sent2,
    got2,
    sent3,
    got3,
    zsent,
    zgot,
    zpart,
    ysent,
    ygot,
    xsent,
    xgot,
    send_sems,
    recv_sems,
    local_sems,
):
    links = Links(send_sems, recv_sems)
    outer, inner = lax.axis_index("outer"), lax.axis_index("inner")
    x, y = lax.rem(outer, NX), lax.div(outer, NX)
    z, c = lax.div(inner, 2), lax.rem(inner, 2)

    def at_x(d):
        return lax.rem(x + d + NX, NX)

    def at_y(d):
        return lax.rem(y + d + NY, NY)

    def at_z(d):
        return lax.rem(z + d + NZ, NZ)

    def to_x(d):
        return place(at_x(d), y, z, c)

    def to_y(d):
        return place(x, at_y(d), z, c)

    def to_z(d):
        return place(x, y, at_z(d), c)

    sibling = place(x, y, z, 1 - c)

    load_tok = pltpu.make_async_copy(tokens, tok.at[pl.ds(0, TOK)], local_sems.at[0])
    load_ups = pltpu.make_async_copy(upstream, ups.at[pl.ds(0, TOK)], local_sems.at[1])
    load_tok.start()
    load_ups.start()

    barrier = pltpu.get_barrier_semaphore()
    partners = [sibling]
    partners += [to_x(d) for d in (1, 2, 3)]
    partners += [to_y(d) for d in (1, 3)]
    partners += [to_z(d) for d in range(1, NZ)]
    for partner in partners:
        pl.semaphore_signal(barrier, inc=1, device_id=partner, device_id_type=MESH)

    row = lax.broadcasted_iota(jnp.int32, (256, 256), 0)
    lane = lax.broadcasted_iota(jnp.int32, (256, 256), 1)
    slot = lane % UNITS
    half = jnp.where(lane < UNITS, c, 1 - c)
    pick = (row == (slot // 16) * 32 + half * 16 + slot % 16).astype(F32).astype(BF16)
    home = y * NX + x
    for m in range(3):
        moved = jnp.dot(shard[m], pick, preferred_element_type=F32).astype(BF16)
        full[m, home, z, pl.ds(pl.multiple_of(c * 32, 32), 32), :] = moved[:, :UNITS]
        stage[m] = moved[:, UNITS:]
    pl.semaphore_wait(barrier, len(partners))

    swap = [
        links.send(
            stage.at[m],
            full.at[m, home, z, pl.ds(pl.multiple_of(c * 32, 32), 32)],
            sibling,
        )
        for m in range(3)
    ]
    for copy in swap:
        copy.wait_recv()
    near = (1, 7, 2, 6, 3, 5, 4)
    block0, block1, block2 = (full.at[m, home, z] for m in range(3))
    a_z = [links.send(block0, block0, to_z(d)) for d in near]
    c_x = [links.send(block2, block2, to_x(d)) for d in (1, 3, 2)]
    b_z = [links.send(block1, block1, to_z(d)) for d in near]
    tok_copy = links.send(tokens, tok.at[pl.ds(TOK, TOK)], sibling)
    ups_copy = links.send(upstream, ups.at[pl.ds(TOK, TOK)], sibling)

    def wait_all(copies):
        for copy in copies:
            copy.wait_recv()

    def plane(yy, zz, x0=0, n=NX):
        return full.at[2, pl.ds(yy * NX + x0, n), zz]

    class Ring4:
        def __init__(self, whole, part, to):
            self.whole, self.part, self.to = whole, part, to

        def first(self):
            ref = self.whole(0)
            self.hop1 = (
                links.send(ref, ref, self.to(1)),
                links.send(ref, ref, self.to(-1)),
            )

        def forward(self):
            wait_all(self.hop1)
            right, left = self.part(-1, 0), self.part(1, 1)
            self.hop2 = (
                links.send(right, right, self.to(1)),
                links.send(left, left, self.to(-1)),
            )

        def finish(self):
            wait_all(self.hop2)

    def piece(m, yy, xx, h=None):
        ref = full.at[m, yy * NX + xx]
        return ref if h is None else ref.at[pl.ds(h * 4, 4)]

    a_y = Ring4(lambda d: piece(0, at_y(d), x), lambda d, h: piece(0, at_y(d), x, h), to_y)
    b_x = Ring4(lambda d: piece(1, y, at_x(d)), lambda d, h: piece(1, y, at_x(d), h), to_x)
    c_y = Ring4(lambda d: plane(at_y(d), z), lambda d, h: plane(at_y(d), z, 2 * h, 2), to_y)

    def a_bulk(g):
        return Ring4(
            lambda d: piece(0, at_y(g), at_x(d)), lambda d, h: piece(0, at_y(g), at_x(d), h), to_x
        )

    def b_bulk(g):
        return Ring4(
            lambda d: piece(1, at_y(d), at_x(g)), lambda d, h: piece(1, at_y(d), at_x(g), h), to_y
        )

    class Ring8:
        def __init__(self, g, long_way):
            self.g, self.hops = g, {1: 4 if long_way == 1 else 3, -1: 4 if long_way == -1 else 3}
            self.last = {}

        def hop(self, h):
            for way in (1, -1):
                if h <= self.hops[way]:
                    if h > 1:
                        self.last[way].wait_recv()
                    ref = plane(at_y(self.g), at_z(-way * (h - 1)))
                    self.last[way] = links.send(ref, ref, to_z(way))

        def finish(self):
            wait_all(self.last.values())

    cz = {g: Ring8(g, 1 if k % 2 == 0 else -1) for k, g in enumerate((0, 1, -1, 2))}
    ax = {g: a_bulk(g) for g in (0, 1, -1, 2)}
    by = {g: b_bulk(g) for g in (0, 1, -1, 2)}

    wait_all(c_x)
    c_y.first()
    cz[0].hop(1)
    wait_all(a_z)
    a_y.first()
    ax[0].first()
    c_y.forward()
    cz[1].hop(1)
    cz[-1].hop(1)
    wait_all(b_z)
    b_x.first()
    by[0].first()
    c_y.finish()
    cz[2].hop(1)
    cz[0].hop(2)
    a_y.forward()
    ax[1].first()
    ax[-1].first()
    b_x.forward()
    by[1].first()
    by[-1].first()
    cz[1].hop(2)
    cz[-1].hop(2)
    ax[0].forward()
    by[0].forward()
    cz[0].hop(3)
    cz[2].hop(2)
    a_y.finish()
    ax[2].first()
    b_x.finish()
    by[2].first()
    cz[1].hop(3)
    cz[-1].hop(3)
    cz[0].hop(4)
    ax[1].forward()
    ax[-1].forward()
    by[1].forward()
    by[-1].forward()
    cz[2].hop(3)
    cz[1].hop(4)
    cz[-1].hop(4)
    ax[2].forward()
    by[2].forward()
    cz[2].hop(4)

    load_tok.wait()
    load_ups.wait()
    tok_copy.wait_recv()

    def forward(m, source):
        def step(k, total):
            rows = pl.ds(pl.multiple_of(k * COLS, COLS), COLS)
            block = full[m, k].reshape(COLS, UNITS)
            return total + jnp.dot(source[:, rows], block, preferred_element_type=F32)

        return lax.fori_loop(0, NX * NY, step, jnp.zeros((2 * TOK, UNITS), F32))

    for g in (0, 1, -1, 2):
        ax[g].finish()
    gate = forward(0, tok)
    for g in (0, 1, -1, 2):
        by[g].finish()
    up = forward(1, tok)
    sigmoid = jax.nn.sigmoid(gate)
    activated = gate * sigmoid
    ups_copy.wait_recv()
    for g in (0, 1, -1, 2):
        cz[g].finish()
    hidden_grad = forward(2, ups)
    hidden = activated * up
    grad_gate = hidden_grad * up * sigmoid * (1.0 + gate * (1.0 - sigmoid))
    grad_up = hidden_grad * activated
    grads[0] = grad_gate.T.astype(BF16)
    grads[1] = grad_up.T.astype(BF16)
    grads[2] = hidden.T.astype(BF16)

    def term(m, yy, xx, h):
        start = pl.multiple_of((yy * NX + xx) * COLS + h * HALF, HALF)
        return jnp.dot(grads[m], tok[:, pl.ds(start, HALF)], preferred_element_type=F32)

    class Fold4:
        def __init__(self, own, sent, got, to):
            self.own, self.sent, self.got, self.to = own, sent, got, to

        def put(self, k, value, way):
            self.sent[k] = value.astype(BF16)
            return links.send(self.sent.at[k], self.got.at[k], self.to(way))

        def far(self):
            self.c0 = self.put(0, self.own(2, 0), 1)
            self.c1 = self.put(1, self.own(2, 1), -1)

        def right(self):
            self.c2 = self.put(2, self.own(1, 1), 1)

        def left(self):
            self.c3 = self.put(3, self.own(-1, 0), -1)

        def relay_right(self):
            self.c0.wait_recv()
            self.c4 = self.put(4, self.own(1, 0) + self.got[0].astype(F32), 1)

        def relay_left(self):
            self.c1.wait_recv()
            self.c5 = self.put(5, self.own(-1, 1) + self.got[1].astype(F32), -1)

        def total(self):
            wait_all((self.c2, self.c3, self.c4, self.c5))
            first = self.own(0, 0) + self.got[4].astype(F32) + self.got[3].astype(F32)
            second = self.own(0, 1) + self.got[2].astype(F32) + self.got[5].astype(F32)
            return first, second

    order = (2, 1, -1, 0)

    def a_fold(k, g):
        return Fold4(
            lambda d, h: term(0, at_y(g), at_x(d), h), sent1.at[0, k], got1.at[0, k], to_x
        )

    def b_fold(k, g):
        return Fold4(
            lambda d, h: term(1, at_y(d), at_x(g), h), sent1.at[1, k], got1.at[1, k], to_y
        )

    folds = [[a_fold(k, g) for k, g in enumerate(order)], [b_fold(k, g) for k, g in enumerate(order)]]
    index = {g: k for k, g in enumerate(order)}

    def half_ref(m, d, h):
        return part1[m, index[2 if d == -2 else d], :, h * HALF : (h + 1) * HALF]

    folds2 = [
        Fold4(lambda d, h: half_ref(0, d, h), sent2.at[0], got2.at[0], to_y),
        Fold4(lambda d, h: half_ref(1, d, h), sent2.at[1], got2.at[1], to_x),
    ]

    def now(k):
        for fold in (folds[0][k], folds[1][k]):
            fold.far()
            fold.right()
            fold.left()

    def relay(k):
        for fold in (folds[0][k], folds[1][k]):
            fold.relay_right()
            fold.relay_left()

    def close(k):
        for m in range(2):
            first, second = folds[m][k].total()
            part1[m, k, :, :HALF] = first
            part1[m, k, :, HALF:] = second

    def c_terms(g):
        base = at_y(g) * NX

        def step(k, carry):
            start = pl.multiple_of((base + k) * COLS, COLS)
            down[:, pl.ds(start, COLS)] = jnp.dot(
                grads[2], ups[:, pl.ds(start, COLS)], preferred_element_type=F32
            )
            return carry

        lax.fori_loop(0, NX, step, 0)

    def c_own(g, d):
        rows = pl.ds(pl.multiple_of(at_z(d) * 16, 16), 16)
        return down[rows, pl.ds(pl.multiple_of(at_y(g) * NX * COLS, NX * COLS), NX * COLS)]

    class Fold8:
        def __init__(self, k, g, long_way):
            self.k, self.g = k, g
            self.hops = {1: 4 if long_way == 1 else 3, -1: 4 if long_way == -1 else 3}
            self.last = {}

        def hop(self, r):
            for w, way in enumerate((1, -1)):
                if r > self.hops[way]:
                    continue
                value = c_own(self.g, way * (self.hops[way] - r + 1))
                if r > 1:
                    self.last[way].wait_recv()
                    value = value + zgot[w, self.k, r - 2].astype(F32)
                zsent[w, self.k, r - 1] = value.astype(BF16)
                self.last[way] = links.send(
                    zsent.at[w, self.k, r - 1], zgot.at[w, self.k, r - 1], to_z(way)
                )

        def close(self):
            wait_all(self.last.values())
            zpart[self.k] = (
                c_own(self.g, 0)
                + zgot[0, self.k, self.hops[1] - 1].astype(F32)
                + zgot[1, self.k, self.hops[-1] - 1].astype(F32)
            )

    zfolds = [Fold8(k, g, 1 if k % 2 == 0 else -1) for k, g in enumerate(order)]

    def wide_half(d, h):
        return zpart[index[d], :, h * NX * HALF : (h + 1) * NX * HALF]

    c_fold2 = Fold4(wide_half, ysent, ygot, to_y)

    def begin_c(k):
        c_terms(order[k])
        zfolds[k].hop(1)

    now(0)
    begin_c(0)
    now(1)
    begin_c(1)
    begin_c(2)
    relay(0)
    begin_c(3)
    now(2)
    zfolds[0].hop(2)
    relay(1)
    zfolds[1].hop(2)
    now(3)
    zfolds[2].hop(2)
    close(0)
    for fold in folds2:
        fold.far()
    zfolds[3].hop(2)
    relay(2)
    zfolds[0].hop(3)
    close(1)
    for fold in folds2:
        fold.right()
    zfolds[1].hop(3)
    relay(3)
    zfolds[2].hop(3)
    close(2)
    for fold in folds2:
        fold.left()
        fold.relay_right()
        fold.relay_left()
    zfolds[3].hop(3)
    zfolds[0].hop(4)
    zfolds[1].hop(4)
    close(3)

    def last_rows(m):
        first, second = folds2[m].total()
        part1[m, 0, :, :HALF] = first
        part1[m, 0, :, HALF:] = second
        sent3[m] = part1[m, 0].astype(BF16)
        copies = []
        for d in (4, 3, 5, 2, 6, 1, 7):
            rows = pl.ds(pl.multiple_of(at_z(d) * 16, 16), 16)
            copies.append(links.send(sent3.at[m, rows], got3.at[m, d - 1], to_z(d)))
        return copies

    third = [last_rows(0), last_rows(1)]
    zfolds[2].hop(4)
    zfolds[3].hop(4)
    zfolds[0].close()
    c_fold2.far()
    zfolds[1].close()
    c_fold2.right()
    zfolds[2].close()
    c_fold2.left()
    c_fold2.relay_right()
    c_fold2.relay_left()
    zfolds[3].close()
    first, second = c_fold2.total()
    zpart[0, :, : NX * HALF] = first
    zpart[0, :, NX * HALF :] = second
    xsent[...] = zpart[0].astype(BF16)

    def columns(d):
        return pl.ds(pl.multiple_of(at_x(d) * COLS, COLS), COLS)

    c_last = [links.send(xsent.at[:, columns(d)], xgot.at[d - 1], to_x(d)) for d in (2, 1, 3)]
    mine = pl.ds(pl.multiple_of(z * 16, 16), 16)
    for m in range(2):
        wait_all(third[m])
        total = part1[m, 0, mine, :]
        for d in range(NZ - 1):
            total = total + got3[m, d].astype(F32)
        out[m] = total
    wait_all(c_last)
    total = zpart[0, :, columns(0)]
    for d in range(NX - 1):
        total = total + xgot[d].astype(F32)
    out[2] = total
    links.drain()


def on_device(tokens, upstream, weights):
    any_space = pl.BlockSpec(memory_space=pl.ANY)
    vmem = pl.BlockSpec(memory_space=pltpu.VMEM)
    dma = pltpu.SemaphoreType.DMA
    return pl.pallas_call(
        kernel,
        out_shape=jax.ShapeDtypeStruct((3, 16, COLS), F32),
        in_specs=[any_space, any_space, vmem],
        out_specs=vmem,
        scratch_shapes=[
            pltpu.VMEM((2 * TOK, MODEL), BF16),
            pltpu.VMEM((2 * TOK, MODEL), BF16),
            pltpu.VMEM((3, NX * NY, NZ, 64, UNITS), BF16),
            pltpu.VMEM((3, 32, UNITS), BF16),
            pltpu.VMEM((3, UNITS, 2 * TOK), BF16),
            pltpu.VMEM((UNITS, MODEL), F32),
            pltpu.VMEM((2, 4, 6, UNITS, HALF), BF16),
            pltpu.VMEM((2, 4, 6, UNITS, HALF), BF16),
            pltpu.VMEM((2, 4, UNITS, COLS), F32),
            pltpu.VMEM((2, 6, UNITS, HALF), BF16),
            pltpu.VMEM((2, 6, UNITS, HALF), BF16),
            pltpu.VMEM((2, UNITS, COLS), BF16),
            pltpu.VMEM((2, NZ - 1, 16, COLS), BF16),
            pltpu.VMEM((2, 4, 4, 16, NX * COLS), BF16),
            pltpu.VMEM((2, 4, 4, 16, NX * COLS), BF16),
            pltpu.VMEM((4, 16, NX * COLS), F32),
            pltpu.VMEM((6, 16, NX * HALF), BF16),
            pltpu.VMEM((6, 16, NX * HALF), BF16),
            pltpu.VMEM((16, NX * COLS), BF16),
            pltpu.VMEM((NX - 1, 16, COLS), BF16),
            dma((N_COPIES,)),
            dma((N_COPIES,)),
            dma((2,)),
        ],
        compiler_params=pltpu.CompilerParams(
            collective_id=0, has_side_effects=True, vmem_limit_bytes=58 << 20
        ),
        name="bucket_grads",
    )(tokens, upstream, weights)


def solution(mesh):
    placed = (
        P(("outer", "inner"), None),
        P(("outer", "inner"), None),
        P(None, ("outer", "inner"), None),
    )
    return jax.shard_map(
        on_device, mesh=mesh, in_specs=placed, out_specs=P(None, "inner", "outer"), check_vma=False
    )
```

```python
import math

import jax
import jax.numpy as jnp
from jax import lax
from jax.experimental import pallas as pl
from jax.experimental.pallas import tpu as pltpu
from jax.sharding import PartitionSpec as P

MESH = pl.DeviceIdType.MESH
BF16, F32 = jnp.bfloat16, jnp.float32
NX, NY, NZ = 4, 4, 8
COLS = 512
HALF = COLS // 2
UNITS = 128
TOK = 256
MODEL = 8192


def place(x, y, z, c):
    return (y * NX + x, z * 2 + c)


class Links:
    def __init__(self, send_sems, recv_sems, measure):
        self.send_sems, self.recv_sems, self.measure = send_sems, recv_sems, measure
        self.used = 0
        self.sent = [0] * N_SENDS

    def group(self):
        self.used += 1
        return [self.used - 1, 0]

    def send(self, group, src, dst, target, lane=0):
        copy = pltpu.make_async_remote_copy(
            src_ref=src,
            dst_ref=dst,
            send_sem=self.send_sems.at[lane],
            recv_sem=self.recv_sems.at[group[0]],
            device_id=target,
            device_id_type=MESH,
        )
        copy.start()
        size = math.prod(src.shape) * 2
        group[1] += size
        self.sent[lane] += size

    def take(self, sem, size):
        rows, rest = divmod(size, ROW)
        assert rest == 0 and rows <= self.measure.shape[0]
        ref = self.measure.at[pl.ds(0, rows)]
        pltpu.make_async_copy(ref, ref, sem).wait()

    def wait(self, group):
        self.take(self.recv_sems.at[group[0]], group[1])

    def drain(self):
        for lane, size in enumerate(self.sent):
            self.take(self.send_sems.at[lane], size)


N_GROUPS = 88
N_SENDS = 4
SUMS = 3
ROW = 64 * UNITS * 2


def kernel(
    tokens,
    upstream,
    shard_hbm,
    out,
    tok,
    ups,
    full,
    stage,
    shard,
    acc,
    acc3,
    grads,
    down,
    held1,
    sent1,
    got1,
    part1,
    held2,
    sent2,
    got2,
    sent3,
    got3,
    zsent,
    zgot,
    zpart,
    yheld,
    ysent,
    ygot,
    xsent,
    xgot,
    send_sems,
    recv_sems,
    local_sems,
):
    links = Links(send_sems, recv_sems, full.reshape(3 * NX * NY * NZ, 64, UNITS))
    outer, inner = lax.axis_index("outer"), lax.axis_index("inner")
    x, y = lax.rem(outer, NX), lax.div(outer, NX)
    z, c = lax.div(inner, 2), lax.rem(inner, 2)

    def at_x(d):
        return lax.rem(x + d + NX, NX)

    def at_y(d):
        return lax.rem(y + d + NY, NY)

    def at_z(d):
        return lax.rem(z + d + NZ, NZ)

    def to_x(d):
        return place(at_x(d), y, z, c)

    def to_y(d):
        return place(x, at_y(d), z, c)

    def to_z(d):
        return place(x, y, at_z(d), c)

    sibling = place(x, y, z, 1 - c)

    load_tok = pltpu.make_async_copy(tokens, tok.at[pl.ds(0, TOK)], local_sems.at[0])
    load_ups = pltpu.make_async_copy(upstream, ups.at[pl.ds(0, TOK)], local_sems.at[1])
    load_shard = pltpu.make_async_copy(shard_hbm, shard, local_sems.at[2])
    load_shard.start()
    load_tok.start()
    load_ups.start()

    barrier = pltpu.get_barrier_semaphore()
    partners = [sibling]
    partners += [to_x(d) for d in (1, 2, 3)]
    partners += [to_y(d) for d in (1, 3)]
    partners += [to_z(d) for d in range(1, NZ)]
    for partner in partners:
        pl.semaphore_signal(barrier, inc=1, device_id=partner, device_id_type=MESH)

    row = lax.broadcasted_iota(jnp.int32, (256, 256), 0)
    lane = lax.broadcasted_iota(jnp.int32, (256, 256), 1)
    slot = lane % UNITS
    half = jnp.where(lane < UNITS, c, 1 - c)
    pick = (row == (slot // 16) * 32 + half * 16 + slot % 16).astype(F32).astype(BF16)
    home = y * NX + x
    load_shard.wait()
    for m in range(3):
        moved = jnp.dot(shard[m], pick, preferred_element_type=F32).astype(BF16)
        full[m, home, z, pl.ds(pl.multiple_of(c * 32, 32), 32), :] = moved[:, :UNITS]
        stage[m] = moved[:, UNITS:]
    pl.semaphore_wait(barrier, len(partners))

    swap = links.group()
    mine_rows = pl.ds(pl.multiple_of(c * 32, 32), 32)
    swap_copy = pltpu.make_async_remote_copy(
        src_ref=stage,
        dst_ref=full.at[:, home, z, mine_rows],
        send_sem=send_sems.at[N_SENDS],
        recv_sem=recv_sems.at[swap[0]],
        device_id=sibling,
        device_id_type=MESH,
    )
    swap_copy.start()
    swap_copy.wait_recv()
    near = (1, 7, 2, 6, 3, 5, 4)
    block0, block1, block2 = (full.at[m, home, z] for m in range(3))
    a_z, b_z, c_x, tok_in, ups_in = (links.group() for _ in range(5))
    for d in near:
        links.send(a_z, block0, block0, to_z(d))
    for d in (1, 3, 2):
        links.send(c_x, block2, block2, to_x(d))
    for d in near:
        links.send(b_z, block1, block1, to_z(d))
    links.send(tok_in, tokens, tok.at[pl.ds(TOK, TOK)], sibling, 1)
    links.send(ups_in, upstream, ups.at[pl.ds(TOK, TOK)], sibling, 2)

    def plane(yy, zz, x0=0, n=NX):
        return full.at[2, pl.ds(yy * NX + x0, n), zz]

    class Ring4:
        def __init__(self, whole, part, to):
            self.whole, self.part, self.to = whole, part, to

        def first(self):
            self.hop1 = links.group()
            ref = self.whole(0)
            links.send(self.hop1, ref, ref, self.to(1))
            links.send(self.hop1, ref, ref, self.to(-1))

        def forward(self):
            links.wait(self.hop1)
            self.hop2 = links.group()
            right, left = self.part(-1, 0), self.part(1, 1)
            links.send(self.hop2, right, right, self.to(1))
            links.send(self.hop2, left, left, self.to(-1))

        def finish(self):
            links.wait(self.hop2)

    def piece(m, yy, xx, h=None):
        ref = full.at[m, yy * NX + xx]
        return ref if h is None else ref.at[pl.ds(h * 4, 4)]

    a_y = Ring4(lambda d: piece(0, at_y(d), x), lambda d, h: piece(0, at_y(d), x, h), to_y)
    b_x = Ring4(lambda d: piece(1, y, at_x(d)), lambda d, h: piece(1, y, at_x(d), h), to_x)
    c_y = Ring4(lambda d: plane(at_y(d), z), lambda d, h: plane(at_y(d), z, 2 * h, 2), to_y)

    def a_bulk(g):
        return Ring4(
            lambda d: piece(0, at_y(g), at_x(d)), lambda d, h: piece(0, at_y(g), at_x(d), h), to_x
        )

    def b_bulk(g):
        return Ring4(
            lambda d: piece(1, at_y(d), at_x(g)), lambda d, h: piece(1, at_y(d), at_x(g), h), to_y
        )

    class Ring8:
        def __init__(self, g, long_way):
            self.g, self.long_way = g, long_way

        def hop(self, h):
            if h > 1:
                links.wait(self.last)
            self.last = links.group()
            for way in (1, -1) if h < 4 else (self.long_way,):
                ref = plane(at_y(self.g), at_z(-way * (h - 1)))
                links.send(self.last, ref, ref, to_z(way))

        def finish(self):
            links.wait(self.last)

    cz = {g: Ring8(g, 1 if k % 2 == 0 else -1) for k, g in enumerate((0, 1, -1, 2))}
    ax = {g: a_bulk(g) for g in (0, 1, -1, 2)}
    by = {g: b_bulk(g) for g in (0, 1, -1, 2)}

    wait = links.wait
    wait(c_x)
    c_y.first()
    cz[0].hop(1)
    wait(a_z)
    a_y.first()
    ax[0].first()
    c_y.forward()
    cz[1].hop(1)
    cz[-1].hop(1)
    wait(b_z)
    b_x.first()
    by[0].first()
    c_y.finish()
    cz[2].hop(1)
    cz[0].hop(2)
    ax[0].forward()
    a_y.forward()
    ax[1].first()
    cz[1].hop(2)
    cz[-1].hop(2)
    b_x.forward()
    ax[-1].first()
    by[1].first()
    by[-1].first()
    by[0].forward()
    cz[2].hop(2)
    a_y.finish()
    ax[2].first()
    cz[0].hop(3)
    ax[1].forward()
    cz[1].hop(3)
    b_x.finish()
    by[2].first()
    cz[-1].hop(3)
    by[1].forward()
    ax[-1].forward()
    cz[2].hop(3)
    by[-1].forward()
    cz[0].hop(4)
    load_tok.wait()
    load_ups.wait()
    wait(tok_in)

    def group_rows(g):
        return pl.ds(pl.multiple_of(at_y(g) * NX * COLS, NX * COLS), NX * COLS)

    def group_block(m, g):
        return full[m, pl.ds(at_y(g) * NX, NX)].reshape(NX * COLS, UNITS)

    def gate_up(g):
        pair = jnp.concatenate([group_block(0, g), group_block(1, g)], axis=1)
        return jnp.dot(tok[:, group_rows(g)], pair, preferred_element_type=F32)

    def third_product(g):
        return jnp.dot(ups[:, group_rows(g)], group_block(2, g), preferred_element_type=F32)

    ax[0].finish()
    acc[...] = gate_up(0)
    cz[1].hop(4)
    cz[-1].hop(4)
    ax[2].forward()
    by[2].forward()
    cz[2].hop(4)
    ax[1].finish()
    acc[...] += gate_up(1)
    ax[-1].finish()
    acc[...] += gate_up(-1)
    wait(ups_in)
    cz[0].finish()
    acc3[...] = third_product(0)
    cz[1].finish()
    acc3[...] += third_product(1)
    cz[-1].finish()
    acc3[...] += third_product(-1)
    ax[2].finish()
    for g in (0, 1, -1, 2):
        by[g].finish()
    acc[...] += gate_up(2)
    cz[2].finish()
    acc3[...] += third_product(2)
    gate, up, hidden_grad = acc[:, :UNITS], acc[:, UNITS:], acc3[...]
    sigmoid = jax.nn.sigmoid(gate)
    activated = gate * sigmoid
    hidden = activated * up
    grad_gate = hidden_grad * up * sigmoid * (1.0 + gate * (1.0 - sigmoid))
    grad_up = hidden_grad * activated
    grads[2] = hidden.T.astype(BF16)
    grads[0] = grad_gate.T.astype(BF16)
    grads[1] = grad_up.T.astype(BF16)

    def term(m, yy, xx):
        start = pl.multiple_of((yy * NX + xx) * COLS, COLS)
        value = jnp.dot(grads[m], tok[:, pl.ds(start, COLS)], preferred_element_type=F32)
        return value[:, :HALF], value[:, HALF:]

    class Fold4:
        def __init__(self, own, held, sent, got, to):
            self.own, self.held, self.sent, self.got, self.to = own, held, sent, got, to

        def put(self, group, k, value, way):
            self.sent[k] = value.astype(BF16)
            links.send(group, self.sent.at[k], self.got.at[k], self.to(way), SUMS)

        def far(self):
            self.hop1, self.hop2 = links.group(), links.group()
            first, second = self.own(2)
            self.put(self.hop1, 0, first, 1)
            self.put(self.hop1, 1, second, -1)

        def right(self):
            first, second = self.own(1)
            self.put(self.hop2, 2, second, 1)
            self.held[0] = first

        def left(self):
            first, second = self.own(-1)
            self.put(self.hop2, 3, first, -1)
            self.held[1] = second

        def relay(self):
            links.wait(self.hop1)
            self.put(self.hop2, 4, self.held[0] + self.got[0].astype(F32), 1)
            self.put(self.hop2, 5, self.held[1] + self.got[1].astype(F32), -1)

        def total(self):
            links.wait(self.hop2)
            first, second = self.own(0)
            first = first + self.got[4].astype(F32) + self.got[3].astype(F32)
            second = second + self.got[2].astype(F32) + self.got[5].astype(F32)
            return first, second

    order = (2, 1, -1, 0)

    def a_fold(k, g):
        own = lambda d: term(0, at_y(g), at_x(d))
        return Fold4(own, held1.at[0, k], sent1.at[0, k], got1.at[0, k], to_x)

    def b_fold(k, g):
        own = lambda d: term(1, at_y(d), at_x(g))
        return Fold4(own, held1.at[1, k], sent1.at[1, k], got1.at[1, k], to_y)

    fa = [a_fold(k, g) for k, g in enumerate(order)]
    fb = [b_fold(k, g) for k, g in enumerate(order)]
    index = {g: k for k, g in enumerate(order)}

    def halves(m, d):
        return part1[m, index[d], :, :HALF], part1[m, index[d], :, HALF:]

    fa2 = Fold4(lambda d: halves(0, d), held2.at[0], sent2.at[0], got2.at[0], to_y)
    fb2 = Fold4(lambda d: halves(1, d), held2.at[1], sent2.at[1], got2.at[1], to_x)

    def close(m, k):
        first, second = (fa, fb)[m][k].total()
        part1[m, k, :, :HALF] = first
        part1[m, k, :, HALF:] = second

    def c_terms(g):
        base = at_y(g) * NX

        def step(k, carry):
            start = pl.multiple_of((base + k) * COLS, COLS)
            down[:, pl.ds(start, COLS)] = jnp.dot(
                grads[2], ups[:, pl.ds(start, COLS)], preferred_element_type=F32
            )
            return carry

        lax.fori_loop(0, NX, step, 0)

    def c_own(g, d):
        rows = pl.ds(pl.multiple_of(at_z(d) * 16, 16), 16)
        return down[rows, pl.ds(pl.multiple_of(at_y(g) * NX * COLS, NX * COLS), NX * COLS)]

    class Fold8:
        def __init__(self, k, g, long_way):
            self.k, self.g = k, g
            self.hops = {1: 4 if long_way == 1 else 3, -1: 4 if long_way == -1 else 3}

        def hop(self, r):
            if r > 1:
                links.wait(self.last)
            self.last = links.group()
            for w, way in enumerate((1, -1)):
                if r > self.hops[way]:
                    continue
                value = c_own(self.g, way * (self.hops[way] - r + 1))
                if r > 1:
                    value = value + zgot[w, self.k, r - 2].astype(F32)
                zsent[w, self.k, r - 1] = value.astype(BF16)
                links.send(
                    self.last, zsent.at[w, self.k, r - 1], zgot.at[w, self.k, r - 1], to_z(way), SUMS
                )

        def close(self):
            links.wait(self.last)
            zpart[self.k] = (
                c_own(self.g, 0)
                + zgot[0, self.k, self.hops[1] - 1].astype(F32)
                + zgot[1, self.k, self.hops[-1] - 1].astype(F32)
            )

    zf = [Fold8(k, g, 1 if k % 2 == 0 else -1) for k, g in enumerate(order)]

    def wide_halves(d):
        return zpart[index[d], :, : NX * HALF], zpart[index[d], :, NX * HALF :]

    fc2 = Fold4(wide_halves, yheld, ysent, ygot, to_y)

    def begin_c(k):
        c_terms(order[k])
        zf[k].hop(1)

    def spread(m):
        first, second = (fa2, fb2)[m].total()
        part1[m, 0, :, :HALF] = first
        part1[m, 0, :, HALF:] = second
        sent3[m] = part1[m, 0].astype(BF16)
        group = links.group()
        for d in (4, 3, 5, 2, 6, 1, 7):
            rows = pl.ds(pl.multiple_of(at_z(d) * 16, 16), 16)
            links.send(group, sent3.at[m, rows], got3.at[m, d - 1], to_z(d), SUMS)
        return group

    begin_c(0)
    fa[0].far()
    fb[0].far()
    begin_c(1)
    fa[0].right()
    fa[0].left()
    fb[0].right()
    fb[0].left()
    begin_c(2)
    zf[0].hop(2)
    fa[0].relay()
    fa[1].far()
    fb[0].relay()
    fb[1].far()
    begin_c(3)
    zf[1].hop(2)
    fa[1].right()
    fa[1].left()
    fb[1].right()
    fb[1].left()
    zf[2].hop(2)
    fa[1].relay()
    fa[2].far()
    fb[1].relay()
    fb[2].far()
    zf[3].hop(2)
    fa[2].right()
    fa[2].left()
    fb[2].right()
    fb[2].left()
    zf[0].hop(3)
    close(0, 0)
    fa2.far()
    close(1, 0)
    fb2.far()
    fa[2].relay()
    fa[3].far()
    fb[2].relay()
    fb[3].far()
    zf[1].hop(3)
    fa[3].right()
    fa[3].left()
    fb[3].right()
    fb[3].left()
    zf[2].hop(3)
    close(0, 1)
    fa2.right()
    close(1, 1)
    fb2.right()
    zf[3].hop(3)
    fa[3].relay()
    fb[3].relay()
    zf[0].hop(4)
    close(0, 2)
    fa2.left()
    fa2.relay()
    close(1, 2)
    fb2.left()
    fb2.relay()
    zf[1].hop(4)
    zf[2].hop(4)
    zf[3].hop(4)
    close(0, 3)
    third0 = spread(0)
    close(1, 3)
    third1 = spread(1)
    zf[0].close()
    fc2.far()
    zf[1].close()
    fc2.right()
    zf[2].close()
    fc2.left()
    fc2.relay()
    zf[3].close()
    first, second = fc2.total()
    zpart[0, :, : NX * HALF] = first
    zpart[0, :, NX * HALF :] = second
    xsent[...] = zpart[0].astype(BF16)

    def columns(d):
        return pl.ds(pl.multiple_of(at_x(d) * COLS, COLS), COLS)

    last = links.group()
    for d in (2, 1, 3):
        links.send(last, xsent.at[:, columns(d)], xgot.at[d - 1], to_x(d), SUMS)
    mine = pl.ds(pl.multiple_of(z * 16, 16), 16)
    for m, group in enumerate((third0, third1)):
        wait(group)
        total = part1[m, 0, mine, :]
        for d in range(NZ - 1):
            total = total + got3[m, d].astype(F32)
        out[m] = total
    wait(last)
    total = zpart[0, :, columns(0)]
    for d in range(NX - 1):
        total = total + xgot[d].astype(F32)
    out[2] = total
    links.drain()
    swap_copy.wait_send()
    assert links.used <= N_GROUPS


def on_device(tokens, upstream, weights):
    any_space = pl.BlockSpec(memory_space=pl.ANY)
    vmem = pl.BlockSpec(memory_space=pltpu.VMEM)
    dma = pltpu.SemaphoreType.DMA
    return pl.pallas_call(
        kernel,
        out_shape=jax.ShapeDtypeStruct((3, 16, COLS), F32),
        in_specs=[any_space, any_space, any_space],
        out_specs=vmem,
        scratch_shapes=[
            pltpu.VMEM((2 * TOK, MODEL), BF16),
            pltpu.VMEM((2 * TOK, MODEL), BF16),
            pltpu.VMEM((3, NX * NY, NZ, 64, UNITS), BF16),
            pltpu.VMEM((3, 32, UNITS), BF16),
            pltpu.VMEM((3, 32, 2 * UNITS), BF16),
            pltpu.VMEM((2 * TOK, 2 * UNITS), F32),
            pltpu.VMEM((2 * TOK, UNITS), F32),
            pltpu.VMEM((3, UNITS, 2 * TOK), BF16),
            pltpu.VMEM((UNITS, MODEL), F32),
            pltpu.VMEM((2, 4, 2, UNITS, HALF), F32),
            pltpu.VMEM((2, 4, 6, UNITS, HALF), BF16),
            pltpu.VMEM((2, 4, 6, UNITS, HALF), BF16),
            pltpu.VMEM((2, 4, UNITS, COLS), F32),
            pltpu.VMEM((2, 2, UNITS, HALF), F32),
            pltpu.VMEM((2, 6, UNITS, HALF), BF16),
            pltpu.VMEM((2, 6, UNITS, HALF), BF16),
            pltpu.VMEM((2, UNITS, COLS), BF16),
            pltpu.VMEM((2, NZ - 1, 16, COLS), BF16),
            pltpu.VMEM((2, 4, 4, 16, NX * COLS), BF16),
            pltpu.VMEM((2, 4, 4, 16, NX * COLS), BF16),
            pltpu.VMEM((4, 16, NX * COLS), F32),
            pltpu.VMEM((2, 16, NX * HALF), F32),
            pltpu.VMEM((6, 16, NX * HALF), BF16),
            pltpu.VMEM((6, 16, NX * HALF), BF16),
            pltpu.VMEM((16, NX * COLS), BF16),
            pltpu.VMEM((NX - 1, 16, COLS), BF16),
            dma((N_SENDS + 1,)),
            dma((N_GROUPS,)),
            dma((3,)),
        ],
        compiler_params=pltpu.CompilerParams(
            collective_id=0, has_side_effects=True, vmem_limit_bytes=58 << 20
        ),
        name="bucket_grads",
    )(tokens, upstream, weights)


def solution(mesh):
    placed = (
        P(("outer", "inner"), None),
        P(("outer", "inner"), None),
        P(None, ("outer", "inner"), None),
    )
    return jax.shard_map(
        on_device, mesh=mesh, in_specs=placed, out_specs=P(None, "inner", "outer"), check_vma=False
    )
```

```python
import functools
import math

import jax
import jax.numpy as jnp
from jax import lax
from jax.experimental import pallas as pl
from jax.experimental.pallas import tpu as pltpu
from jax.sharding import PartitionSpec as P

MESH = pl.DeviceIdType.MESH
BF16, F32 = jnp.bfloat16, jnp.float32
NX, NY, NZ = 4, 4, 8
COLS = 512
HALF = COLS // 2
UNITS = 128
TOK = 256
MODEL = 8192


def place(x, y, z, c):
    return (y * NX + x, z * 2 + c)


ORDER = (
    0, 11, 1, 3, 7, 2, 27, 19,
    9, 5, 40, 12, 4, 23, 8, 15,
    35, 28, 20, 6, 42, 17, 41, 10,
    45, 13, 50, 25, 31, 36, 24, 29,
    18, 51, 21, 55, 14, 16, 46, 37,
    33, 43, 26, 47, 30, 52, 22, 32,
    56, 39, 34, 53, 38, 44, 48, 57,
    49, 58, 59, 113, 118, 119, 115, 54,
    60, 87, 61, 88, 76, 92, 94, 93,
    66, 62, 89, 114, 120, 95, 121, 90,
    77, 71, 67, 116, 123, 124, 125, 63,
    97, 99, 78, 98, 122, 91, 107, 117,
    72, 133, 134, 126, 100, 68, 128, 130,
    64, 129, 102, 103, 104, 79, 96, 108,
    127, 135, 136, 73, 131, 101, 109, 110,
    69, 105, 80, 65, 81, 74, 132, 137,
    70, 82, 106, 75, 83, 111, 84, 138,
    85, 86, 112,
)


class Links:
    def __init__(self, send_sems, recv_sems, measure):
        self.send_sems, self.recv_sems, self.measure = send_sems, recv_sems, measure
        self.used = 0
        self.sent = [0] * N_SENDS

    def group(self):
        self.used += 1
        return [self.used - 1, 0, False]

    def send(self, group, src, dst, target, lane=0):
        copy = pltpu.make_async_remote_copy(
            src_ref=src,
            dst_ref=dst,
            send_sem=self.send_sems.at[lane],
            recv_sem=self.recv_sems.at[group[0]],
            device_id=target,
            device_id_type=MESH,
        )
        copy.start()
        size = math.prod(src.shape) * 2
        group[1] += size
        self.sent[lane] += size

    def take(self, sem, size):
        rows, rest = divmod(size, ROW)
        assert rest == 0 and rows <= self.measure.shape[0]
        ref = self.measure.at[pl.ds(0, rows)]
        pltpu.make_async_copy(ref, ref, sem).wait()

    def wait(self, group):
        if not group[2]:
            group[2] = True
            self.take(self.recv_sems.at[group[0]], group[1])

    def drain(self):
        for lane, size in enumerate(self.sent):
            self.take(self.send_sems.at[lane], size)


ROLES = ("z", "yx", "xy")
N_GROUPS = 88
N_SENDS = 4
SUMS = 3
ROW = 64 * UNITS * 2


def kernel(
    tokens,
    upstream,
    shard_hbm,
    out,
    tok,
    ups,
    full,
    stage,
    shard,
    acc,
    acc3,
    grads,
    factors,
    zterms,
    held1,
    sent1,
    got1,
    part1,
    held2,
    sent2,
    got2,
    last1,
    sent3,
    got3,
    zsent,
    zgot,
    zpart,
    yheld,
    ysent,
    ygot,
    last2,
    xsent,
    xgot,
    send_sems,
    recv_sems,
    local_sems,
):
    links = Links(send_sems, recv_sems, full.reshape(3 * NX * NY * NZ, 64, UNITS))
    outer, inner = lax.axis_index("outer"), lax.axis_index("inner")
    x, y = lax.rem(outer, NX), lax.div(outer, NX)
    z, c = lax.div(inner, 2), lax.rem(inner, 2)

    def at_x(d):
        return lax.rem(x + d + NX, NX)

    def at_y(d):
        return lax.rem(y + d + NY, NY)

    def at_z(d):
        return lax.rem(z + d + NZ, NZ)

    def to_x(d):
        return place(at_x(d), y, z, c)

    def to_y(d):
        return place(x, at_y(d), z, c)

    def to_z(d):
        return place(x, y, at_z(d), c)

    sibling = place(x, y, z, 1 - c)

    load_tok = pltpu.make_async_copy(tokens, tok.at[pl.ds(0, TOK)], local_sems.at[0])
    load_ups = pltpu.make_async_copy(upstream, ups.at[pl.ds(0, TOK)], local_sems.at[1])
    load_shard = pltpu.make_async_copy(shard_hbm, shard, local_sems.at[2])
    load_shard.start()
    load_tok.start()
    load_ups.start()

    barrier = pltpu.get_barrier_semaphore()
    partners = [sibling]
    partners += [to_x(d) for d in (1, 2, 3)]
    partners += [to_y(d) for d in (1, 3)]
    partners += [to_z(d) for d in range(1, NZ)]
    for partner in partners:
        pl.semaphore_signal(barrier, inc=1, device_id=partner, device_id_type=MESH)

    row = lax.broadcasted_iota(jnp.int32, (256, 256), 0)
    lane = lax.broadcasted_iota(jnp.int32, (256, 256), 1)
    slot = lane % UNITS
    half = jnp.where(lane < UNITS, c, 1 - c)
    pick = (row == (slot // 16) * 32 + half * 16 + slot % 16).astype(F32).astype(BF16)
    home = y * NX + x
    load_shard.wait()
    for m in range(3):
        moved = jnp.dot(shard[m], pick, preferred_element_type=F32).astype(BF16)
        full[m, home, z, pl.ds(pl.multiple_of(c * 32, 32), 32), :] = moved[:, :UNITS]
        stage[m] = moved[:, UNITS:]
    pl.semaphore_wait(barrier, len(partners))

    swap = links.group()
    mine_rows = pl.ds(pl.multiple_of(c * 32, 32), 32)
    swap_copy = pltpu.make_async_remote_copy(
        src_ref=stage,
        dst_ref=full.at[:, home, z, mine_rows],
        send_sem=send_sems.at[N_SENDS],
        recv_sem=recv_sems.at[swap[0]],
        device_id=sibling,
        device_id_type=MESH,
    )
    swap_copy.start()
    swap_copy.wait_recv()
    near = (1, 7, 2, 6, 3, 5, 4)
    block0, block1, block2 = (full.at[m, home, z] for m in range(3))
    a_z, b_z, c_x, tok_in, ups_in = (links.group() for _ in range(5))
    for d in near:
        links.send(a_z, block0, block0, to_z(d))
    for d in (1, 3, 2):
        links.send(c_x, block2, block2, to_x(d))
    for d in near:
        links.send(b_z, block1, block1, to_z(d))
    links.send(tok_in, tokens, tok.at[pl.ds(TOK, TOK)], sibling, 1)
    links.send(ups_in, upstream, ups.at[pl.ds(TOK, TOK)], sibling, 2)

    def plane(yy, zz, x0=0, n=NX):
        return full.at[2, pl.ds(yy * NX + x0, n), zz]

    class Ring4:
        def __init__(self, whole, part, to, ready):
            self.whole, self.part, self.to, self.ready = whole, part, to, ready

        def first(self):
            for group in self.ready():
                links.wait(group)
            self.hop1 = links.group()
            ref = self.whole(0)
            links.send(self.hop1, ref, ref, self.to(1))
            links.send(self.hop1, ref, ref, self.to(-1))

        def forward(self):
            links.wait(self.hop1)
            self.hop2 = links.group()
            right, left = self.part(-1, 0), self.part(1, 1)
            links.send(self.hop2, right, right, self.to(1))
            links.send(self.hop2, left, left, self.to(-1))

        def finish(self):
            links.wait(self.hop2)

    def piece(m, yy, xx, h=None):
        ref = full.at[m, yy * NX + xx]
        return ref if h is None else ref.at[pl.ds(h * 4, 4)]

    a_y = Ring4(
        lambda d: piece(0, at_y(d), x), lambda d, h: piece(0, at_y(d), x, h), to_y, lambda: (a_z,)
    )
    b_x = Ring4(
        lambda d: piece(1, y, at_x(d)), lambda d, h: piece(1, y, at_x(d), h), to_x, lambda: (b_z,)
    )
    c_y = Ring4(
        lambda d: plane(at_y(d), z), lambda d, h: plane(at_y(d), z, 2 * h, 2), to_y, lambda: (c_x,)
    )

    def whole_block(start, ring, g):
        return (start,) if g == 0 else (ring.hop2,) if g == 2 else (ring.hop1,)

    def a_bulk(g):
        return Ring4(
            lambda d: piece(0, at_y(g), at_x(d)),
            lambda d, h: piece(0, at_y(g), at_x(d), h),
            to_x,
            lambda: whole_block(a_z, a_y, g),
        )

    def b_bulk(g):
        return Ring4(
            lambda d: piece(1, at_y(d), at_x(g)),
            lambda d, h: piece(1, at_y(d), at_x(g), h),
            to_y,
            lambda: whole_block(b_z, b_x, g),
        )

    class Ring8:
        def __init__(self, g, long_way):
            self.g, self.long_way = g, long_way

        def hop(self, h):
            for group in (self.last,) if h > 1 else whole_block(c_x, c_y, self.g):
                links.wait(group)
            self.last = links.group()
            for way in (1, -1) if h < 4 else (self.long_way,):
                ref = plane(at_y(self.g), at_z(-way * (h - 1)))
                links.send(self.last, ref, ref, to_z(way))

        def finish(self):
            links.wait(self.last)

    cz = {g: Ring8(g, 1 if k % 2 == 0 else -1) for k, g in enumerate((0, 1, -1, 2))}
    ax = {g: a_bulk(g) for g in (0, 1, -1, 2)}
    by = {g: b_bulk(g) for g in (0, 1, -1, 2)}

    wait = links.wait
    steps = [lambda: None]
    for ring in (c_y, a_y, b_x):
        steps += [ring.first, ring.forward]
    for g in (0, 1, -1, 2):
        for ring in (ax[g], by[g]):
            steps += [ring.first, ring.forward]
        steps += [functools.partial(cz[g].hop, h) for h in (1, 2, 3, 4)]

    done = set()

    def once(key, action):
        if key not in done:
            done.add(key)
            action()

    def gate_up(dy, dx):
        once("tok", load_tok.wait)
        wait(tok_in)
        at0 = ax[dy].hop2 if dx == 2 else ax[dy].hop1 if dx else whole_block(a_z, a_y, dy)[0]
        at1 = by[dx].hop2 if dy == 2 else by[dx].hop1 if dy else whole_block(b_z, b_x, dx)[0]
        wait(at0)
        wait(at1)
        k = at_y(dy) * NX + at_x(dx)
        pair = jnp.concatenate([full[m, k].reshape(COLS, UNITS) for m in range(2)], axis=1)
        rows = pl.ds(pl.multiple_of(k * COLS, COLS), COLS)
        value = jnp.dot(tok[:, rows], pair, preferred_element_type=F32)
        if "gate_up" in done:
            acc[...] += value
        else:
            acc[...] = value
        done.add("gate_up")

    def third_product(g):
        once("ups", load_ups.wait)
        wait(ups_in)
        cz[g].finish()
        rows = pl.ds(pl.multiple_of(at_y(g) * NX * COLS, NX * COLS), NX * COLS)
        block = full[2, pl.ds(at_y(g) * NX, NX)].reshape(NX * COLS, UNITS)
        value = jnp.dot(ups[:, rows], block, preferred_element_type=F32)
        if "third" in done:
            acc3[...] += value
        else:
            acc3[...] = value
        done.add("third")

    def activate():
        gate, up = acc[:, :UNITS], acc[:, UNITS:]
        sigmoid = jax.nn.sigmoid(gate)
        activated = gate * sigmoid
        grads[2] = (activated * up).astype(BF16).T
        factors[1] = activated
        factors[0] = up * sigmoid * (1.0 + gate * (1.0 - sigmoid))

    def differentiate():
        hidden_grad = acc3[...]
        for m in range(2):
            grads[m] = (hidden_grad * factors[m]).astype(BF16).T

    for dy in (0, 1, -1, 2):
        steps.append(functools.partial(third_product, dy))
        steps += [functools.partial(gate_up, dy, dx) for dx in (0, 1, -1, 2)]
    steps += [activate, differentiate]

    def term(m, yy, xx):
        start = pl.multiple_of((yy * NX + xx) * COLS, COLS)
        source = ups if m == 2 else tok
        value = jnp.dot(grads[m], source[:, pl.ds(start, COLS)], preferred_element_type=F32)
        return value[:, :HALF], value[:, HALF:]

    class Fold4:
        def __init__(self, own, held, sent, got, to):
            self.own, self.held, self.sent, self.got, self.to = own, held, sent, got, to

        def steps(self):
            return [self.far, self.right, self.left, self.relay]

        def put(self, group, k, value, way):
            self.sent[k] = value.astype(BF16)
            links.send(group, self.sent.at[k], self.got.at[k], self.to(way), SUMS)

        def far(self):
            self.hop1, self.hop2 = links.group(), links.group()
            first, second = self.own(2)
            self.put(self.hop1, 0, first, 1)
            self.put(self.hop1, 1, second, -1)

        def right(self):
            first, second = self.own(1)
            self.put(self.hop2, 2, second, 1)
            self.held[0] = first

        def left(self):
            first, second = self.own(-1)
            self.put(self.hop2, 3, first, -1)
            self.held[1] = second

        def relay(self):
            links.wait(self.hop1)
            self.put(self.hop2, 4, self.held[0] + self.got[0].astype(F32), 1)
            self.put(self.hop2, 5, self.held[1] + self.got[1].astype(F32), -1)

        def total(self):
            links.wait(self.hop2)
            first, second = self.own(0)
            first = first + self.got[4].astype(F32) + self.got[3].astype(F32)
            second = second + self.got[2].astype(F32) + self.got[5].astype(F32)
            return first, second

    order = (2, 1, -1, 0)
    index = {g: k for k, g in enumerate(order)}
    mine = pl.ds(pl.multiple_of(z * 16, 16), 16)

    class Sums:
        def __init__(self, slot, m, x_first):
            self.m, self.slot = m, slot
            to1, to2 = (to_x, to_y) if x_first else (to_y, to_x)

            def own(g, d):
                return term(m, at_y(g), at_x(d)) if x_first else term(m, at_y(d), at_x(g))

            self.folds = [
                Fold4(
                    functools.partial(own, g),
                    held1.at[slot, k],
                    sent1.at[slot, k],
                    got1.at[slot, k],
                    to1,
                )
                for k, g in enumerate(order)
            ]
            self.second = Fold4(self.halves, held2.at[slot], sent2.at[slot], got2.at[slot], to2)
            self.steps = []
            for k, fold in enumerate(self.folds):
                self.steps += fold.steps() + [functools.partial(self.close, k)]
            self.steps += self.second.steps() + [self.spread, self.out]

        def halves(self, d):
            k = index[d]
            return part1[self.slot, k, :, :HALF], part1[self.slot, k, :, HALF:]

        def close(self, k):
            first, second = self.folds[k].total()
            part1[self.slot, k, :, :HALF] = first
            part1[self.slot, k, :, HALF:] = second

        def spread(self):
            slot = self.slot
            first, second = self.second.total()
            last1[slot, :, :HALF] = first
            last1[slot, :, HALF:] = second
            sent3[slot] = last1[slot].astype(BF16)
            self.last = links.group()
            for d in (4, 3, 5, 2, 6, 1, 7):
                rows = pl.ds(pl.multiple_of(at_z(d) * 16, 16), 16)
                links.send(self.last, sent3.at[slot, rows], got3.at[slot, d - 1], to_z(d), SUMS)

        def out(self):
            wait(self.last)
            total = last1[self.slot, mine, :]
            for d in range(NZ - 1):
                total = total + got3[self.slot, d].astype(F32)
            out[self.m] = total

    class Fold8:
        def __init__(self, m, k, g, long_way):
            self.m, self.k, self.g = m, k, g
            self.hops = {1: 4 if long_way == 1 else 3, -1: 4 if long_way == -1 else 3}

        def terms(self):
            source, base = (ups if self.m == 2 else tok), at_y(self.g) * NX

            def step(k, carry):
                start = pl.multiple_of((base + k) * COLS, COLS)
                zterms[:, pl.ds(start, COLS)] = jnp.dot(
                    grads[self.m], source[:, pl.ds(start, COLS)], preferred_element_type=F32
                )
                return carry

            lax.fori_loop(0, NX, step, 0)

        def own(self, d):
            rows = pl.ds(pl.multiple_of(at_z(d) * 16, 16), 16)
            width = NX * COLS
            return zterms[rows, pl.ds(pl.multiple_of(at_y(self.g) * width, width), width)]

        def hop(self, r):
            if r == 1:
                self.terms()
            else:
                wait(self.last)
            self.last = links.group()
            for w, way in enumerate((1, -1)):
                if r > self.hops[way]:
                    continue
                value = self.own(way * (self.hops[way] - r + 1))
                if r > 1:
                    value = value + zgot[w, self.k, r - 2].astype(F32)
                zsent[w, self.k, r - 1] = value.astype(BF16)
                links.send(
                    self.last, zsent.at[w, self.k, r - 1], zgot.at[w, self.k, r - 1], to_z(way), SUMS
                )

        def close(self):
            wait(self.last)
            zpart[self.k] = (
                self.own(0)
                + zgot[0, self.k, self.hops[1] - 1].astype(F32)
                + zgot[1, self.k, self.hops[-1] - 1].astype(F32)
            )

    class ZSums:
        def __init__(self, m):
            self.m = m
            self.folds = [Fold8(m, k, g, 1 if k % 2 == 0 else -1) for k, g in enumerate(order)]
            self.second = Fold4(self.halves, yheld, ysent, ygot, to_y)
            self.steps = []
            for fold in self.folds:
                self.steps += [functools.partial(fold.hop, r) for r in (1, 2, 3, 4)] + [fold.close]
            self.steps += self.second.steps() + [self.spread, self.out]

        def halves(self, d):
            return zpart[index[d], :, : NX * HALF], zpart[index[d], :, NX * HALF :]

        def columns(self, d):
            return pl.ds(pl.multiple_of(at_x(d) * COLS, COLS), COLS)

        def spread(self):
            first, second = self.second.total()
            last2[:, : NX * HALF] = first
            last2[:, NX * HALF :] = second
            xsent[...] = last2[...].astype(BF16)
            self.last = links.group()
            for d in (2, 1, 3):
                links.send(self.last, xsent.at[:, self.columns(d)], xgot.at[d - 1], to_x(d), SUMS)

        def out(self):
            wait(self.last)
            total = last2[:, self.columns(0)]
            for d in range(NX - 1):
                total = total + xgot[d].astype(F32)
            out[self.m] = total

    slot = 0
    for m in range(3):
        if ROLES[m] == "z":
            steps += ZSums(m).steps
        else:
            steps += Sums(slot, m, ROLES[m] == "xy").steps
            slot += 1

    assert sorted(ORDER) == list(range(len(steps)))
    for number in ORDER:
        steps[number]()
    links.drain()
    swap_copy.wait_send()
    assert links.used <= N_GROUPS


def on_device(tokens, upstream, weights):
    any_space = pl.BlockSpec(memory_space=pl.ANY)
    vmem = pl.BlockSpec(memory_space=pltpu.VMEM)
    dma = pltpu.SemaphoreType.DMA
    return pl.pallas_call(
        kernel,
        out_shape=jax.ShapeDtypeStruct((3, 16, COLS), F32),
        in_specs=[any_space, any_space, any_space],
        out_specs=vmem,
        scratch_shapes=[
            pltpu.VMEM((2 * TOK, MODEL), BF16),
            pltpu.VMEM((2 * TOK, MODEL), BF16),
            pltpu.VMEM((3, NX * NY, NZ, 64, UNITS), BF16),
            pltpu.VMEM((3, 32, UNITS), BF16),
            pltpu.VMEM((3, 32, 2 * UNITS), BF16),
            pltpu.VMEM((2 * TOK, 2 * UNITS), F32),
            pltpu.VMEM((2 * TOK, UNITS), F32),
            pltpu.VMEM((3, UNITS, 2 * TOK), BF16),
            pltpu.VMEM((2, 2 * TOK, UNITS), F32),
            pltpu.VMEM((UNITS, MODEL), F32),
            pltpu.VMEM((2, 4, 2, UNITS, HALF), F32),
            pltpu.VMEM((2, 4, 6, UNITS, HALF), BF16),
            pltpu.VMEM((2, 4, 6, UNITS, HALF), BF16),
            pltpu.VMEM((2, 4, UNITS, COLS), F32),
            pltpu.VMEM((2, 2, UNITS, HALF), F32),
            pltpu.VMEM((2, 6, UNITS, HALF), BF16),
            pltpu.VMEM((2, 6, UNITS, HALF), BF16),
            pltpu.VMEM((2, UNITS, COLS), F32),
            pltpu.VMEM((2, UNITS, COLS), BF16),
            pltpu.VMEM((2, NZ - 1, 16, COLS), BF16),
            pltpu.VMEM((2, 4, 4, 16, NX * COLS), BF16),
            pltpu.VMEM((2, 4, 4, 16, NX * COLS), BF16),
            pltpu.VMEM((4, 16, NX * COLS), F32),
            pltpu.VMEM((2, 16, NX * HALF), F32),
            pltpu.VMEM((6, 16, NX * HALF), BF16),
            pltpu.VMEM((6, 16, NX * HALF), BF16),
            pltpu.VMEM((16, NX * COLS), F32),
            pltpu.VMEM((16, NX * COLS), BF16),
            pltpu.VMEM((NX - 1, 16, COLS), BF16),
            dma((N_SENDS + 1,)),
            dma((N_GROUPS,)),
            dma((3,)),
        ],
        compiler_params=pltpu.CompilerParams(
            collective_id=0, has_side_effects=True, vmem_limit_bytes=58 << 20
        ),
        name="bucket_grads",
    )(tokens, upstream, weights)


def solution(mesh):
    placed = (
        P(("outer", "inner"), None),
        P(("outer", "inner"), None),
        P(None, ("outer", "inner"), None),
    )
    return jax.shard_map(
        on_device, mesh=mesh, in_specs=placed, out_specs=P(None, "inner", "outer"), check_vma=False
    )
```

```python
import functools
import math

import jax
import jax.numpy as jnp
from jax import lax
from jax.experimental import pallas as pl
from jax.experimental.pallas import tpu as pltpu
from jax.sharding import PartitionSpec as P

MESH = pl.DeviceIdType.MESH
BF16, F32 = jnp.bfloat16, jnp.float32
NX, NY, NZ = 4, 4, 8
COLS = 512
HALF = COLS // 2
UNITS = 128
TOK = 256
MODEL = 8192


def place(x, y, z, c):
    return (y * NX + x, z * 2 + c)


ORDER = (
    0, 1, 11, 3, 7, 5, 9, 2,
    27, 19, 12, 40, 8, 4, 23, 15,
    28, 6, 17, 41, 10, 45, 35, 42,
    25, 13, 20, 50, 31, 29, 24, 36,
    51, 18, 14, 55, 46, 16, 21, 33,
    43, 30, 26, 52, 47, 37, 56, 32,
    39, 22, 34, 53, 48, 49, 57, 38,
    44, 58, 59, 123, 124, 118, 119, 120,
    54, 60, 76, 87, 89, 88, 92, 61,
    121, 102, 66, 90, 71, 113, 114, 115,
    62, 97, 98, 99, 67, 93, 125, 91,
    126, 72, 116, 94, 63, 95, 100, 107,
    104, 77, 68, 103, 105, 122, 128, 73,
    130, 127, 129, 64, 117, 133, 134, 96,
    108, 78, 135, 101, 109, 110, 69, 131,
    74, 106, 65, 81, 136, 79, 70, 82,
    111, 75, 83, 84, 132, 137, 80, 85,
    112, 86, 138,
)


class Links:
    def __init__(self, send_sems, recv_sems, measure):
        self.send_sems, self.recv_sems, self.measure = send_sems, recv_sems, measure
        self.used = 0
        self.sent = [0] * N_SENDS

    def group(self):
        self.used += 1
        return [self.used - 1, 0, False]

    def send(self, group, src, dst, target, lane=0):
        copy = pltpu.make_async_remote_copy(
            src_ref=src,
            dst_ref=dst,
            send_sem=self.send_sems.at[lane],
            recv_sem=self.recv_sems.at[group[0]],
            device_id=target,
            device_id_type=MESH,
        )
        copy.start()
        size = math.prod(src.shape) * 2
        group[1] += size
        self.sent[lane] += size

    def take(self, sem, size):
        rows, rest = divmod(size, ROW)
        assert rest == 0 and rows <= self.measure.shape[0]
        ref = self.measure.at[pl.ds(0, rows)]
        pltpu.make_async_copy(ref, ref, sem).wait()

    def wait(self, group):
        if not group[2]:
            group[2] = True
            self.take(self.recv_sems.at[group[0]], group[1])

    def drain(self):
        for lane, size in enumerate(self.sent):
            self.take(self.send_sems.at[lane], size)


ROLES = ("z", "yx", "xy")
N_GROUPS = 88
N_SENDS = 4
SUMS = 3
ROW = 64 * UNITS * 2


def kernel(
    tokens,
    upstream,
    shard_hbm,
    out,
    tok,
    ups,
    full,
    stage,
    shard,
    acc,
    acc3,
    grads,
    factors,
    zterms,
    held1,
    sent1,
    got1,
    part1,
    held2,
    sent2,
    got2,
    last1,
    sent3,
    got3,
    zsent,
    zgot,
    zpart,
    yheld,
    ysent,
    ygot,
    last2,
    xsent,
    xgot,
    send_sems,
    recv_sems,
    local_sems,
):
    links = Links(send_sems, recv_sems, full.reshape(3 * NX * NY * NZ, 64, UNITS))
    outer, inner = lax.axis_index("outer"), lax.axis_index("inner")
    x, y = lax.rem(outer, NX), lax.div(outer, NX)
    z, c = lax.div(inner, 2), lax.rem(inner, 2)

    def at_x(d):
        return lax.rem(x + d + NX, NX)

    def at_y(d):
        return lax.rem(y + d + NY, NY)

    def at_z(d):
        return lax.rem(z + d + NZ, NZ)

    def to_x(d):
        return place(at_x(d), y, z, c)

    def to_y(d):
        return place(x, at_y(d), z, c)

    def to_z(d):
        return place(x, y, at_z(d), c)

    sibling = place(x, y, z, 1 - c)

    load_tok = pltpu.make_async_copy(tokens, tok.at[pl.ds(0, TOK)], local_sems.at[0])
    load_ups = pltpu.make_async_copy(upstream, ups.at[pl.ds(0, TOK)], local_sems.at[1])
    load_shard = pltpu.make_async_copy(shard_hbm, shard, local_sems.at[2])
    load_shard.start()
    load_tok.start()
    load_ups.start()

    barrier = pltpu.get_barrier_semaphore()
    partners = [sibling]
    partners += [to_x(d) for d in (1, 2, 3)]
    partners += [to_y(d) for d in (1, 3)]
    partners += [to_z(d) for d in range(1, NZ)]
    for partner in partners:
        pl.semaphore_signal(barrier, inc=1, device_id=partner, device_id_type=MESH)

    row = lax.broadcasted_iota(jnp.int32, (256, 256), 0)
    lane = lax.broadcasted_iota(jnp.int32, (256, 256), 1)
    slot = lane % UNITS
    half = jnp.where(lane < UNITS, c, 1 - c)
    pick = (row == (slot // 16) * 32 + half * 16 + slot % 16).astype(F32).astype(BF16)
    home = y * NX + x
    load_shard.wait()
    for m in range(3):
        moved = jnp.dot(shard[m], pick, preferred_element_type=F32).astype(BF16)
        full[m, home, z, pl.ds(pl.multiple_of(c * 32, 32), 32), :] = moved[:, :UNITS]
        stage[m] = moved[:, UNITS:]
    pl.semaphore_wait(barrier, len(partners))

    swap = links.group()
    mine_rows = pl.ds(pl.multiple_of(c * 32, 32), 32)
    swap_copy = pltpu.make_async_remote_copy(
        src_ref=stage,
        dst_ref=full.at[:, home, z, mine_rows],
        send_sem=send_sems.at[N_SENDS],
        recv_sem=recv_sems.at[swap[0]],
        device_id=sibling,
        device_id_type=MESH,
    )
    swap_copy.start()
    near = (1, 7, 2, 6, 3, 5, 4)
    a_z, b_z, c_x, tok_in, ups_in = (links.group() for _ in range(5))
    own_rows, other_rows = mine_rows, pl.ds(pl.multiple_of((1 - c) * 32, 32), 32)

    def start(group, m, targets, rows):
        ref = full.at[m, home, z, rows]
        for target in targets:
            links.send(group, ref, ref, target)

    along_z, along_x = [to_z(d) for d in near], [to_x(d) for d in (1, 3, 2)]
    start(a_z, 0, along_z, own_rows)
    start(c_x, 2, along_x, own_rows)
    swap_copy.wait_recv()
    start(a_z, 0, along_z, other_rows)
    start(c_x, 2, along_x, other_rows)
    start(b_z, 1, along_z, own_rows)
    start(b_z, 1, along_z, other_rows)
    links.send(tok_in, tokens, tok.at[pl.ds(TOK, TOK)], sibling, 1)
    links.send(ups_in, upstream, ups.at[pl.ds(TOK, TOK)], sibling, 2)

    def plane(yy, zz, x0=0, n=NX):
        return full.at[2, pl.ds(yy * NX + x0, n), zz]

    class Ring4:
        def __init__(self, whole, part, to, ready):
            self.whole, self.part, self.to, self.ready = whole, part, to, ready

        def first(self):
            for group in self.ready():
                links.wait(group)
            self.hop1 = links.group()
            ref = self.whole(0)
            links.send(self.hop1, ref, ref, self.to(1))
            links.send(self.hop1, ref, ref, self.to(-1))

        def forward(self):
            links.wait(self.hop1)
            self.hop2 = links.group()
            right, left = self.part(-1, 0), self.part(1, 1)
            links.send(self.hop2, right, right, self.to(1))
            links.send(self.hop2, left, left, self.to(-1))

        def finish(self):
            links.wait(self.hop2)

    def piece(m, yy, xx, h=None):
        ref = full.at[m, yy * NX + xx]
        return ref if h is None else ref.at[pl.ds(h * 4, 4)]

    a_y = Ring4(
        lambda d: piece(0, at_y(d), x), lambda d, h: piece(0, at_y(d), x, h), to_y, lambda: (a_z,)
    )
    b_x = Ring4(
        lambda d: piece(1, y, at_x(d)), lambda d, h: piece(1, y, at_x(d), h), to_x, lambda: (b_z,)
    )
    c_y = Ring4(
        lambda d: plane(at_y(d), z), lambda d, h: plane(at_y(d), z, 2 * h, 2), to_y, lambda: (c_x,)
    )

    def whole_block(start, ring, g):
        return (start,) if g == 0 else (ring.hop2,) if g == 2 else (ring.hop1,)

    def a_bulk(g):
        return Ring4(
            lambda d: piece(0, at_y(g), at_x(d)),
            lambda d, h: piece(0, at_y(g), at_x(d), h),
            to_x,
            lambda: whole_block(a_z, a_y, g),
        )

    def b_bulk(g):
        return Ring4(
            lambda d: piece(1, at_y(d), at_x(g)),
            lambda d, h: piece(1, at_y(d), at_x(g), h),
            to_y,
            lambda: whole_block(b_z, b_x, g),
        )

    class Ring8:
        def __init__(self, g, long_way):
            self.g, self.long_way = g, long_way

        def hop(self, h):
            for group in (self.last,) if h > 1 else whole_block(c_x, c_y, self.g):
                links.wait(group)
            self.last = links.group()
            for way in (1, -1) if h < 4 else (self.long_way,):
                ref = plane(at_y(self.g), at_z(-way * (h - 1)))
                links.send(self.last, ref, ref, to_z(way))

        def finish(self):
            links.wait(self.last)

    cz = {g: Ring8(g, 1 if k % 2 == 0 else -1) for k, g in enumerate((0, 1, -1, 2))}
    ax = {g: a_bulk(g) for g in (0, 1, -1, 2)}
    by = {g: b_bulk(g) for g in (0, 1, -1, 2)}

    wait = links.wait
    steps = [lambda: None]
    for ring in (c_y, a_y, b_x):
        steps += [ring.first, ring.forward]
    for g in (0, 1, -1, 2):
        for ring in (ax[g], by[g]):
            steps += [ring.first, ring.forward]
        steps += [functools.partial(cz[g].hop, h) for h in (1, 2, 3, 4)]

    done = set()

    def once(key, action):
        if key not in done:
            done.add(key)
            action()

    def gate_up(dy, dx):
        once("tok", load_tok.wait)
        wait(tok_in)
        at0 = ax[dy].hop2 if dx == 2 else ax[dy].hop1 if dx else whole_block(a_z, a_y, dy)[0]
        at1 = by[dx].hop2 if dy == 2 else by[dx].hop1 if dy else whole_block(b_z, b_x, dx)[0]
        wait(at0)
        wait(at1)
        k = at_y(dy) * NX + at_x(dx)
        pair = jnp.concatenate([full[m, k].reshape(COLS, UNITS) for m in range(2)], axis=1)
        rows = pl.ds(pl.multiple_of(k * COLS, COLS), COLS)
        value = jnp.dot(tok[:, rows], pair, preferred_element_type=F32)
        if "gate_up" in done:
            acc[...] += value
        else:
            acc[...] = value
        done.add("gate_up")

    def third_product(g):
        once("ups", load_ups.wait)
        wait(ups_in)
        cz[g].finish()
        rows = pl.ds(pl.multiple_of(at_y(g) * NX * COLS, NX * COLS), NX * COLS)
        block = full[2, pl.ds(at_y(g) * NX, NX)].reshape(NX * COLS, UNITS)
        value = jnp.dot(ups[:, rows], block, preferred_element_type=F32)
        if "third" in done:
            acc3[...] += value
        else:
            acc3[...] = value
        done.add("third")

    def activate():
        gate, up = acc[:, :UNITS], acc[:, UNITS:]
        sigmoid = jax.nn.sigmoid(gate)
        activated = gate * sigmoid
        grads[2] = (activated * up).astype(BF16).T
        factors[1] = activated
        factors[0] = up * sigmoid * (1.0 + gate * (1.0 - sigmoid))

    def differentiate():
        hidden_grad = acc3[...]
        for m in range(2):
            grads[m] = (hidden_grad * factors[m]).astype(BF16).T

    for dy in (0, 1, -1, 2):
        steps.append(functools.partial(third_product, dy))
        steps += [functools.partial(gate_up, dy, dx) for dx in (0, 1, -1, 2)]
    steps += [activate, differentiate]

    def term(m, yy, xx):
        start = pl.multiple_of((yy * NX + xx) * COLS, COLS)
        source = ups if m == 2 else tok
        value = jnp.dot(grads[m], source[:, pl.ds(start, COLS)], preferred_element_type=F32)
        return value[:, :HALF], value[:, HALF:]

    class Fold4:
        def __init__(self, own, held, sent, got, to):
            self.own, self.held, self.sent, self.got, self.to = own, held, sent, got, to

        def steps(self):
            return [self.far, self.right, self.left, self.relay]

        def put(self, group, k, value, way):
            self.sent[k] = value.astype(BF16)
            links.send(group, self.sent.at[k], self.got.at[k], self.to(way), SUMS)

        def far(self):
            self.hop1, self.hop2 = links.group(), links.group()
            first, second = self.own(2)
            self.put(self.hop1, 0, first, 1)
            self.put(self.hop1, 1, second, -1)

        def right(self):
            first, second = self.own(1)
            self.put(self.hop2, 2, second, 1)
            self.held[0] = first

        def left(self):
            first, second = self.own(-1)
            self.put(self.hop2, 3, first, -1)
            self.held[1] = second

        def relay(self):
            links.wait(self.hop1)
            self.put(self.hop2, 4, self.held[0] + self.got[0].astype(F32), 1)
            self.put(self.hop2, 5, self.held[1] + self.got[1].astype(F32), -1)

        def total(self):
            links.wait(self.hop2)
            first, second = self.own(0)
            first = first + self.got[4].astype(F32) + self.got[3].astype(F32)
            second = second + self.got[2].astype(F32) + self.got[5].astype(F32)
            return first, second

    order = (2, 1, -1, 0)
    index = {g: k for k, g in enumerate(order)}
    mine = pl.ds(pl.multiple_of(z * 16, 16), 16)

    class Sums:
        def __init__(self, slot, m, x_first):
            self.m, self.slot = m, slot
            to1, to2 = (to_x, to_y) if x_first else (to_y, to_x)

            def own(g, d):
                return term(m, at_y(g), at_x(d)) if x_first else term(m, at_y(d), at_x(g))

            self.folds = [
                Fold4(
                    functools.partial(own, g),
                    held1.at[slot, k],
                    sent1.at[slot, k],
                    got1.at[slot, k],
                    to1,
                )
                for k, g in enumerate(order)
            ]
            self.second = Fold4(self.halves, held2.at[slot], sent2.at[slot], got2.at[slot], to2)
            self.steps = []
            for k, fold in enumerate(self.folds):
                self.steps += fold.steps() + [functools.partial(self.close, k)]
            self.steps += self.second.steps() + [self.spread, self.out]

        def halves(self, d):
            k = index[d]
            return part1[self.slot, k, :, :HALF], part1[self.slot, k, :, HALF:]

        def close(self, k):
            first, second = self.folds[k].total()
            part1[self.slot, k, :, :HALF] = first
            part1[self.slot, k, :, HALF:] = second

        def spread(self):
            slot = self.slot
            first, second = self.second.total()
            last1[slot, :, :HALF] = first
            last1[slot, :, HALF:] = second
            sent3[slot] = last1[slot].astype(BF16)
            self.last = links.group()
            for d in (4, 3, 5, 2, 6, 1, 7):
                rows = pl.ds(pl.multiple_of(at_z(d) * 16, 16), 16)
                links.send(self.last, sent3.at[slot, rows], got3.at[slot, d - 1], to_z(d), SUMS)

        def out(self):
            wait(self.last)
            total = last1[self.slot, mine, :]
            for d in range(NZ - 1):
                total = total + got3[self.slot, d].astype(F32)
            out[self.m] = total

    class Fold8:
        def __init__(self, m, k, g, long_way):
            self.m, self.k, self.g = m, k, g
            self.hops = {1: 4 if long_way == 1 else 3, -1: 4 if long_way == -1 else 3}

        def terms(self):
            source, base = (ups if self.m == 2 else tok), at_y(self.g) * NX

            def step(k, carry):
                start = pl.multiple_of((base + k) * COLS, COLS)
                zterms[:, pl.ds(start, COLS)] = jnp.dot(
                    grads[self.m], source[:, pl.ds(start, COLS)], preferred_element_type=F32
                )
                return carry

            lax.fori_loop(0, NX, step, 0)

        def own(self, d):
            rows = pl.ds(pl.multiple_of(at_z(d) * 16, 16), 16)
            width = NX * COLS
            return zterms[rows, pl.ds(pl.multiple_of(at_y(self.g) * width, width), width)]

        def hop(self, r):
            if r == 1:
                self.terms()
            else:
                wait(self.last)
            self.last = links.group()
            for w, way in enumerate((1, -1)):
                if r > self.hops[way]:
                    continue
                value = self.own(way * (self.hops[way] - r + 1))
                if r > 1:
                    value = value + zgot[w, self.k, r - 2].astype(F32)
                zsent[w, self.k, r - 1] = value.astype(BF16)
                links.send(
                    self.last, zsent.at[w, self.k, r - 1], zgot.at[w, self.k, r - 1], to_z(way), SUMS
                )

        def close(self):
            wait(self.last)
            zpart[self.k] = (
                self.own(0)
                + zgot[0, self.k, self.hops[1] - 1].astype(F32)
                + zgot[1, self.k, self.hops[-1] - 1].astype(F32)
            )

    class ZSums:
        def __init__(self, m):
            self.m = m
            self.folds = [Fold8(m, k, g, 1 if k % 2 == 0 else -1) for k, g in enumerate(order)]
            self.second = Fold4(self.halves, yheld, ysent, ygot, to_y)
            self.steps = []
            for fold in self.folds:
                self.steps += [functools.partial(fold.hop, r) for r in (1, 2, 3, 4)] + [fold.close]
            self.steps += self.second.steps() + [self.spread, self.out]

        def halves(self, d):
            return zpart[index[d], :, : NX * HALF], zpart[index[d], :, NX * HALF :]

        def columns(self, d):
            return pl.ds(pl.multiple_of(at_x(d) * COLS, COLS), COLS)

        def spread(self):
            first, second = self.second.total()
            last2[:, : NX * HALF] = first
            last2[:, NX * HALF :] = second
            xsent[...] = last2[...].astype(BF16)
            self.last = links.group()
            for d in (2, 1, 3):
                links.send(self.last, xsent.at[:, self.columns(d)], xgot.at[d - 1], to_x(d), SUMS)

        def out(self):
            wait(self.last)
            total = last2[:, self.columns(0)]
            for d in range(NX - 1):
                total = total + xgot[d].astype(F32)
            out[self.m] = total

    slot = 0
    for m in range(3):
        if ROLES[m] == "z":
            steps += ZSums(m).steps
        else:
            steps += Sums(slot, m, ROLES[m] == "xy").steps
            slot += 1

    assert sorted(ORDER) == list(range(len(steps)))
    for number in ORDER:
        steps[number]()
    links.drain()
    swap_copy.wait_send()
    assert links.used <= N_GROUPS


def on_device(tokens, upstream, weights):
    any_space = pl.BlockSpec(memory_space=pl.ANY)
    vmem = pl.BlockSpec(memory_space=pltpu.VMEM)
    dma = pltpu.SemaphoreType.DMA
    return pl.pallas_call(
        kernel,
        out_shape=jax.ShapeDtypeStruct((3, 16, COLS), F32),
        in_specs=[any_space, any_space, any_space],
        out_specs=vmem,
        scratch_shapes=[
            pltpu.VMEM((2 * TOK, MODEL), BF16),
            pltpu.VMEM((2 * TOK, MODEL), BF16),
            pltpu.VMEM((3, NX * NY, NZ, 64, UNITS), BF16),
            pltpu.VMEM((3, 32, UNITS), BF16),
            pltpu.VMEM((3, 32, 2 * UNITS), BF16),
            pltpu.VMEM((2 * TOK, 2 * UNITS), F32),
            pltpu.VMEM((2 * TOK, UNITS), F32),
            pltpu.VMEM((3, UNITS, 2 * TOK), BF16),
            pltpu.VMEM((2, 2 * TOK, UNITS), F32),
            pltpu.VMEM((UNITS, MODEL), F32),
            pltpu.VMEM((2, 4, 2, UNITS, HALF), F32),
            pltpu.VMEM((2, 4, 6, UNITS, HALF), BF16),
            pltpu.VMEM((2, 4, 6, UNITS, HALF), BF16),
            pltpu.VMEM((2, 4, UNITS, COLS), F32),
            pltpu.VMEM((2, 2, UNITS, HALF), F32),
            pltpu.VMEM((2, 6, UNITS, HALF), BF16),
            pltpu.VMEM((2, 6, UNITS, HALF), BF16),
            pltpu.VMEM((2, UNITS, COLS), F32),
            pltpu.VMEM((2, UNITS, COLS), BF16),
            pltpu.VMEM((2, NZ - 1, 16, COLS), BF16),
            pltpu.VMEM((2, 4, 4, 16, NX * COLS), BF16),
            pltpu.VMEM((2, 4, 4, 16, NX * COLS), BF16),
            pltpu.VMEM((4, 16, NX * COLS), F32),
            pltpu.VMEM((2, 16, NX * HALF), F32),
            pltpu.VMEM((6, 16, NX * HALF), BF16),
            pltpu.VMEM((6, 16, NX * HALF), BF16),
            pltpu.VMEM((16, NX * COLS), F32),
            pltpu.VMEM((16, NX * COLS), BF16),
            pltpu.VMEM((NX - 1, 16, COLS), BF16),
            dma((N_SENDS + 1,)),
            dma((N_GROUPS,)),
            dma((3,)),
        ],
        compiler_params=pltpu.CompilerParams(
            collective_id=0, has_side_effects=True, vmem_limit_bytes=58 << 20
        ),
        name="bucket_grads",
    )(tokens, upstream, weights)


def solution(mesh):
    placed = (
        P(("outer", "inner"), None),
        P(("outer", "inner"), None),
        P(None, ("outer", "inner"), None),
    )
    return jax.shard_map(
        on_device, mesh=mesh, in_specs=placed, out_specs=P(None, "inner", "outer"), check_vma=False
    )
```

```python
import functools
import math

import jax
import jax.numpy as jnp
from jax import lax
from jax.experimental import pallas as pl
from jax.experimental.pallas import tpu as pltpu
from jax.sharding import PartitionSpec as P

MESH = pl.DeviceIdType.MESH
BF16, F32 = jnp.bfloat16, jnp.float32
NX, NY, NZ = 4, 4, 8
COLS = 512
HALF = COLS // 2
UNITS = 128
TOK = 256
MODEL = 8192


def place(x, y, z, c):
    return (y * NX + x, z * 2 + c)


ORDER = (
    0, 1, 11, 3, 7, 5, 9, 2,
    27, 19, 12, 40, 8, 4, 23, 15,
    28, 6, 17, 41, 10, 45, 35, 42,
    25, 13, 20, 50, 31, 29, 24, 36,
    51, 18, 14, 55, 46, 16, 21, 33,
    43, 30, 26, 52, 47, 37, 56, 32,
    39, 22, 34, 53, 48, 49, 57, 38,
    44, 58, 59, 123, 124, 118, 119, 120,
    54, 60, 76, 87, 89, 88, 92, 61,
    121, 102, 66, 90, 71, 113, 114, 115,
    62, 97, 98, 99, 67, 93, 125, 91,
    126, 72, 116, 94, 63, 95, 100, 107,
    104, 77, 68, 103, 105, 122, 128, 73,
    130, 127, 129, 64, 117, 133, 134, 96,
    108, 78, 135, 101, 109, 110, 69, 131,
    74, 106, 65, 81, 136, 79, 70, 82,
    111, 75, 83, 84, 132, 137, 80, 85,
    112, 86, 138,
)


class Links:
    def __init__(self, send_sems, recv_sems, measure):
        self.send_sems, self.recv_sems, self.measure = send_sems, recv_sems, measure
        self.used = 0
        self.sent = [0] * N_SENDS

    def group(self):
        self.used += 1
        return [self.used - 1, 0, False]

    def send(self, group, src, dst, target, lane=0):
        copy = pltpu.make_async_remote_copy(
            src_ref=src,
            dst_ref=dst,
            send_sem=self.send_sems.at[lane],
            recv_sem=self.recv_sems.at[group[0]],
            device_id=target,
            device_id_type=MESH,
        )
        copy.start()
        size = math.prod(src.shape) * 2
        group[1] += size
        self.sent[lane] += size

    def take(self, sem, size):
        rows, rest = divmod(size, ROW)
        assert rest == 0 and rows <= self.measure.shape[0]
        ref = self.measure.at[pl.ds(0, rows)]
        pltpu.make_async_copy(ref, ref, sem).wait()

    def wait(self, group):
        if not group[2]:
            group[2] = True
            self.take(self.recv_sems.at[group[0]], group[1])

    def drain(self):
        for lane, size in enumerate(self.sent):
            self.take(self.send_sems.at[lane], size)


ROLES = ("z", "yx", "xy")
N_GROUPS = 88
N_SENDS = 4
SUMS = 3
ROW = 64 * UNITS * 2


def kernel(
    tokens,
    upstream,
    shard_hbm,
    out,
    tok,
    ups,
    full,
    stage,
    shard,
    acc,
    acc3,
    grads,
    factors,
    zterms,
    held1,
    sent1,
    got1,
    part1,
    held2,
    sent2,
    got2,
    last1,
    sent3,
    got3,
    zsent,
    zgot,
    zpart,
    yheld,
    ysent,
    ygot,
    last2,
    xsent,
    xgot,
    send_sems,
    recv_sems,
    local_sems,
):
    links = Links(send_sems, recv_sems, full.reshape(3 * NX * NY * NZ, 64, UNITS))
    outer, inner = lax.axis_index("outer"), lax.axis_index("inner")
    x, y = lax.rem(outer, NX), lax.div(outer, NX)
    z, c = lax.div(inner, 2), lax.rem(inner, 2)

    def at_x(d):
        return lax.rem(x + d + NX, NX)

    def at_y(d):
        return lax.rem(y + d + NY, NY)

    def at_z(d):
        return lax.rem(z + d + NZ, NZ)

    def to_x(d):
        return place(at_x(d), y, z, c)

    def to_y(d):
        return place(x, at_y(d), z, c)

    def to_z(d):
        return place(x, y, at_z(d), c)

    sibling = place(x, y, z, 1 - c)

    load_tok = pltpu.make_async_copy(tokens, tok.at[pl.ds(0, TOK)], local_sems.at[0])
    load_ups = pltpu.make_async_copy(upstream, ups.at[pl.ds(0, TOK)], local_sems.at[1])
    load_shard = pltpu.make_async_copy(shard_hbm, shard, local_sems.at[2])
    load_shard.start()
    load_tok.start()
    load_ups.start()

    barrier = pltpu.get_barrier_semaphore()
    partners = [sibling]
    partners += [to_x(d) for d in (1, 2, 3)]
    partners += [to_y(d) for d in (1, 3)]
    partners += [to_z(d) for d in range(1, NZ)]
    for partner in partners:
        pl.semaphore_signal(barrier, inc=1, device_id=partner, device_id_type=MESH)

    row = lax.broadcasted_iota(jnp.int32, (256, 256), 0)
    lane = lax.broadcasted_iota(jnp.int32, (256, 256), 1)
    slot = lane % UNITS
    half = jnp.where(lane < UNITS, c, 1 - c)
    pick = (row == (slot // 16) * 32 + half * 16 + slot % 16).astype(F32).astype(BF16)
    home = y * NX + x
    load_shard.wait()
    for m in range(3):
        moved = jnp.dot(shard[m], pick, preferred_element_type=F32).astype(BF16)
        full[m, home, z, pl.ds(pl.multiple_of(c * 32, 32), 32), :] = moved[:, :UNITS]
        stage[m] = moved[:, UNITS:]
    pl.semaphore_wait(barrier, len(partners))

    swap = links.group()
    mine_rows = pl.ds(pl.multiple_of(c * 32, 32), 32)
    swap_copy = pltpu.make_async_remote_copy(
        src_ref=stage,
        dst_ref=full.at[:, home, z, mine_rows],
        send_sem=send_sems.at[N_SENDS],
        recv_sem=recv_sems.at[swap[0]],
        device_id=sibling,
        device_id_type=MESH,
    )
    swap_copy.start()
    near = (4, 3, 5, 2, 6, 1, 7)
    a_z, b_z, c_x, tok_in, ups_in = (links.group() for _ in range(5))
    own_rows, other_rows = mine_rows, pl.ds(pl.multiple_of((1 - c) * 32, 32), 32)

    def start(group, m, targets, rows):
        ref = full.at[m, home, z, rows]
        for target in targets:
            links.send(group, ref, ref, target)

    along_z, along_x = [to_z(d) for d in near], [to_x(d) for d in (1, 3, 2)]
    start(c_x, 2, along_x, own_rows)
    start(a_z, 0, along_z, own_rows)
    swap_copy.wait_recv()
    start(a_z, 0, along_z, other_rows)
    start(c_x, 2, along_x, other_rows)
    start(b_z, 1, along_z, own_rows)
    start(b_z, 1, along_z, other_rows)
    links.send(tok_in, tokens, tok.at[pl.ds(TOK, TOK)], sibling, 1)
    links.send(ups_in, upstream, ups.at[pl.ds(TOK, TOK)], sibling, 2)

    def plane(yy, zz, x0=0, n=NX):
        return full.at[2, pl.ds(yy * NX + x0, n), zz]

    class Ring4:
        def __init__(self, whole, part, to, ready):
            self.whole, self.part, self.to, self.ready = whole, part, to, ready

        def first(self):
            for group in self.ready():
                links.wait(group)
            self.hop1 = links.group()
            ref = self.whole(0)
            links.send(self.hop1, ref, ref, self.to(1))
            links.send(self.hop1, ref, ref, self.to(-1))

        def forward(self):
            links.wait(self.hop1)
            self.hop2 = links.group()
            right, left = self.part(-1, 0), self.part(1, 1)
            links.send(self.hop2, right, right, self.to(1))
            links.send(self.hop2, left, left, self.to(-1))

        def finish(self):
            links.wait(self.hop2)

    def piece(m, yy, xx, h=None):
        ref = full.at[m, yy * NX + xx]
        return ref if h is None else ref.at[pl.ds(h * 4, 4)]

    a_y = Ring4(
        lambda d: piece(0, at_y(d), x), lambda d, h: piece(0, at_y(d), x, h), to_y, lambda: (a_z,)
    )
    b_x = Ring4(
        lambda d: piece(1, y, at_x(d)), lambda d, h: piece(1, y, at_x(d), h), to_x, lambda: (b_z,)
    )
    c_y = Ring4(
        lambda d: plane(at_y(d), z), lambda d, h: plane(at_y(d), z, 2 * h, 2), to_y, lambda: (c_x,)
    )

    def whole_block(start, ring, g):
        return (start,) if g == 0 else (ring.hop2,) if g == 2 else (ring.hop1,)

    def a_bulk(g):
        return Ring4(
            lambda d: piece(0, at_y(g), at_x(d)),
            lambda d, h: piece(0, at_y(g), at_x(d), h),
            to_x,
            lambda: whole_block(a_z, a_y, g),
        )

    def b_bulk(g):
        return Ring4(
            lambda d: piece(1, at_y(d), at_x(g)),
            lambda d, h: piece(1, at_y(d), at_x(g), h),
            to_y,
            lambda: whole_block(b_z, b_x, g),
        )

    class Ring8:
        def __init__(self, g, long_way):
            self.g, self.long_way = g, long_way

        def hop(self, h):
            for group in (self.last,) if h > 1 else whole_block(c_x, c_y, self.g):
                links.wait(group)
            self.last = links.group()
            for way in (1, -1) if h < 4 else (self.long_way,):
                ref = plane(at_y(self.g), at_z(-way * (h - 1)))
                links.send(self.last, ref, ref, to_z(way))

        def finish(self):
            links.wait(self.last)

    cz = {g: Ring8(g, 1 if k % 2 == 0 else -1) for k, g in enumerate((0, 1, -1, 2))}
    ax = {g: a_bulk(g) for g in (0, 1, -1, 2)}
    by = {g: b_bulk(g) for g in (0, 1, -1, 2)}

    wait = links.wait
    steps = [lambda: None]
    for ring in (c_y, a_y, b_x):
        steps += [ring.first, ring.forward]
    for g in (0, 1, -1, 2):
        for ring in (ax[g], by[g]):
            steps += [ring.first, ring.forward]
        steps += [functools.partial(cz[g].hop, h) for h in (1, 2, 3, 4)]

    done = set()

    def once(key, action):
        if key not in done:
            done.add(key)
            action()

    def gate_up(dy, dx):
        once("tok", load_tok.wait)
        wait(tok_in)
        at0 = ax[dy].hop2 if dx == 2 else ax[dy].hop1 if dx else whole_block(a_z, a_y, dy)[0]
        at1 = by[dx].hop2 if dy == 2 else by[dx].hop1 if dy else whole_block(b_z, b_x, dx)[0]
        wait(at0)
        wait(at1)
        k = at_y(dy) * NX + at_x(dx)
        pair = jnp.concatenate([full[m, k].reshape(COLS, UNITS) for m in range(2)], axis=1)
        rows = pl.ds(pl.multiple_of(k * COLS, COLS), COLS)
        value = jnp.dot(tok[:, rows], pair, preferred_element_type=F32)
        if "gate_up" in done:
            acc[...] += value
        else:
            acc[...] = value
        done.add("gate_up")

    def third_product(g):
        once("ups", load_ups.wait)
        wait(ups_in)
        cz[g].finish()
        rows = pl.ds(pl.multiple_of(at_y(g) * NX * COLS, NX * COLS), NX * COLS)
        block = full[2, pl.ds(at_y(g) * NX, NX)].reshape(NX * COLS, UNITS)
        value = jnp.dot(ups[:, rows], block, preferred_element_type=F32)
        if "third" in done:
            acc3[...] += value
        else:
            acc3[...] = value
        done.add("third")

    def activate():
        gate, up = acc[:, :UNITS], acc[:, UNITS:]
        sigmoid = jax.nn.sigmoid(gate)
        activated = gate * sigmoid
        grads[2] = (activated * up).astype(BF16).T
        factors[1] = activated
        factors[0] = up * sigmoid * (1.0 + gate * (1.0 - sigmoid))

    def differentiate():
        hidden_grad = acc3[...]
        for m in range(2):
            grads[m] = (hidden_grad * factors[m]).astype(BF16).T

    for dy in (0, 1, -1, 2):
        steps.append(functools.partial(third_product, dy))
        steps += [functools.partial(gate_up, dy, dx) for dx in (0, 1, -1, 2)]
    steps += [activate, differentiate]

    def term(m, yy, xx):
        start = pl.multiple_of((yy * NX + xx) * COLS, COLS)
        source = ups if m == 2 else tok
        value = jnp.dot(grads[m], source[:, pl.ds(start, COLS)], preferred_element_type=F32)
        return value[:, :HALF], value[:, HALF:]

    class Fold4:
        def __init__(self, own, held, sent, got, to):
            self.own, self.held, self.sent, self.got, self.to = own, held, sent, got, to

        def steps(self):
            return [self.far, self.right, self.left, self.relay]

        def put(self, group, k, value, way):
            self.sent[k] = value.astype(BF16)
            links.send(group, self.sent.at[k], self.got.at[k], self.to(way), SUMS)

        def far(self):
            self.hop1, self.hop2 = links.group(), links.group()
            first, second = self.own(2)
            self.put(self.hop1, 0, first, 1)
            self.put(self.hop1, 1, second, -1)

        def right(self):
            first, second = self.own(1)
            self.put(self.hop2, 2, second, 1)
            self.held[0] = first

        def left(self):
            first, second = self.own(-1)
            self.put(self.hop2, 3, first, -1)
            self.held[1] = second

        def relay(self):
            links.wait(self.hop1)
            self.put(self.hop2, 4, self.held[0] + self.got[0].astype(F32), 1)
            self.put(self.hop2, 5, self.held[1] + self.got[1].astype(F32), -1)

        def total(self):
            links.wait(self.hop2)
            first, second = self.own(0)
            first = first + self.got[4].astype(F32) + self.got[3].astype(F32)
            second = second + self.got[2].astype(F32) + self.got[5].astype(F32)
            return first, second

    order = (2, 1, -1, 0)
    index = {g: k for k, g in enumerate(order)}
    mine = pl.ds(pl.multiple_of(z * 16, 16), 16)

    class Sums:
        def __init__(self, slot, m, x_first):
            self.m, self.slot = m, slot
            to1, to2 = (to_x, to_y) if x_first else (to_y, to_x)

            def own(g, d):
                return term(m, at_y(g), at_x(d)) if x_first else term(m, at_y(d), at_x(g))

            self.folds = [
                Fold4(
                    functools.partial(own, g),
                    held1.at[slot, k],
                    sent1.at[slot, k],
                    got1.at[slot, k],
                    to1,
                )
                for k, g in enumerate(order)
            ]
            self.second = Fold4(self.halves, held2.at[slot], sent2.at[slot], got2.at[slot], to2)
            self.steps = []
            for k, fold in enumerate(self.folds):
                self.steps += fold.steps() + [functools.partial(self.close, k)]
            self.steps += self.second.steps() + [self.spread, self.out]

        def halves(self, d):
            k = index[d]
            return part1[self.slot, k, :, :HALF], part1[self.slot, k, :, HALF:]

        def close(self, k):
            first, second = self.folds[k].total()
            part1[self.slot, k, :, :HALF] = first
            part1[self.slot, k, :, HALF:] = second

        def spread(self):
            slot = self.slot
            first, second = self.second.total()
            last1[slot, :, :HALF] = first
            last1[slot, :, HALF:] = second
            sent3[slot] = last1[slot].astype(BF16)
            self.last = links.group()
            for d in (4, 3, 5, 2, 6, 1, 7):
                rows = pl.ds(pl.multiple_of(at_z(d) * 16, 16), 16)
                links.send(self.last, sent3.at[slot, rows], got3.at[slot, d - 1], to_z(d), SUMS)

        def out(self):
            wait(self.last)
            total = last1[self.slot, mine, :]
            for d in range(NZ - 1):
                total = total + got3[self.slot, d].astype(F32)
            out[self.m] = total

    class Fold8:
        def __init__(self, m, k, g, long_way):
            self.m, self.k, self.g = m, k, g
            self.hops = {1: 4 if long_way == 1 else 3, -1: 4 if long_way == -1 else 3}

        def terms(self):
            source, base = (ups if self.m == 2 else tok), at_y(self.g) * NX

            def step(k, carry):
                start = pl.multiple_of((base + k) * COLS, COLS)
                zterms[:, pl.ds(start, COLS)] = jnp.dot(
                    grads[self.m], source[:, pl.ds(start, COLS)], preferred_element_type=F32
                )
                return carry

            lax.fori_loop(0, NX, step, 0)

        def own(self, d):
            rows = pl.ds(pl.multiple_of(at_z(d) * 16, 16), 16)
            width = NX * COLS
            return zterms[rows, pl.ds(pl.multiple_of(at_y(self.g) * width, width), width)]

        def hop(self, r):
            if r == 1:
                self.terms()
            else:
                wait(self.last)
            self.last = links.group()
            for w, way in enumerate((1, -1)):
                if r > self.hops[way]:
                    continue
                value = self.own(way * (self.hops[way] - r + 1))
                if r > 1:
                    value = value + zgot[w, self.k, r - 2].astype(F32)
                zsent[w, self.k, r - 1] = value.astype(BF16)
                links.send(
                    self.last, zsent.at[w, self.k, r - 1], zgot.at[w, self.k, r - 1], to_z(way), SUMS
                )

        def close(self):
            wait(self.last)
            zpart[self.k] = (
                self.own(0)
                + zgot[0, self.k, self.hops[1] - 1].astype(F32)
                + zgot[1, self.k, self.hops[-1] - 1].astype(F32)
            )

    class ZSums:
        def __init__(self, m):
            self.m = m
            self.folds = [Fold8(m, k, g, 1 if k % 2 == 0 else -1) for k, g in enumerate(order)]
            self.second = Fold4(self.halves, yheld, ysent, ygot, to_y)
            self.steps = []
            for fold in self.folds:
                self.steps += [functools.partial(fold.hop, r) for r in (1, 2, 3, 4)] + [fold.close]
            self.steps += self.second.steps() + [self.spread, self.out]

        def halves(self, d):
            return zpart[index[d], :, : NX * HALF], zpart[index[d], :, NX * HALF :]

        def columns(self, d):
            return pl.ds(pl.multiple_of(at_x(d) * COLS, COLS), COLS)

        def spread(self):
            first, second = self.second.total()
            last2[:, : NX * HALF] = first
            last2[:, NX * HALF :] = second
            xsent[...] = last2[...].astype(BF16)
            self.last = links.group()
            for d in (2, 1, 3):
                links.send(self.last, xsent.at[:, self.columns(d)], xgot.at[d - 1], to_x(d), SUMS)

        def out(self):
            wait(self.last)
            total = last2[:, self.columns(0)]
            for d in range(NX - 1):
                total = total + xgot[d].astype(F32)
            out[self.m] = total

    slot = 0
    for m in range(3):
        if ROLES[m] == "z":
            steps += ZSums(m).steps
        else:
            steps += Sums(slot, m, ROLES[m] == "xy").steps
            slot += 1

    assert sorted(ORDER) == list(range(len(steps)))
    for number in ORDER:
        steps[number]()
    links.drain()
    swap_copy.wait_send()
    assert links.used <= N_GROUPS


def on_device(tokens, upstream, weights):
    any_space = pl.BlockSpec(memory_space=pl.ANY)
    vmem = pl.BlockSpec(memory_space=pltpu.VMEM)
    dma = pltpu.SemaphoreType.DMA
    return pl.pallas_call(
        kernel,
        out_shape=jax.ShapeDtypeStruct((3, 16, COLS), F32),
        in_specs=[any_space, any_space, any_space],
        out_specs=vmem,
        scratch_shapes=[
            pltpu.VMEM((2 * TOK, MODEL), BF16),
            pltpu.VMEM((2 * TOK, MODEL), BF16),
            pltpu.VMEM((3, NX * NY, NZ, 64, UNITS), BF16),
            pltpu.VMEM((3, 32, UNITS), BF16),
            pltpu.VMEM((3, 32, 2 * UNITS), BF16),
            pltpu.VMEM((2 * TOK, 2 * UNITS), F32),
            pltpu.VMEM((2 * TOK, UNITS), F32),
            pltpu.VMEM((3, UNITS, 2 * TOK), BF16),
            pltpu.VMEM((2, 2 * TOK, UNITS), F32),
            pltpu.VMEM((UNITS, MODEL), F32),
            pltpu.VMEM((2, 4, 2, UNITS, HALF), F32),
            pltpu.VMEM((2, 4, 6, UNITS, HALF), BF16),
            pltpu.VMEM((2, 4, 6, UNITS, HALF), BF16),
            pltpu.VMEM((2, 4, UNITS, COLS), F32),
            pltpu.VMEM((2, 2, UNITS, HALF), F32),
            pltpu.VMEM((2, 6, UNITS, HALF), BF16),
            pltpu.VMEM((2, 6, UNITS, HALF), BF16),
            pltpu.VMEM((2, UNITS, COLS), F32),
            pltpu.VMEM((2, UNITS, COLS), BF16),
            pltpu.VMEM((2, NZ - 1, 16, COLS), BF16),
            pltpu.VMEM((2, 4, 4, 16, NX * COLS), BF16),
            pltpu.VMEM((2, 4, 4, 16, NX * COLS), BF16),
            pltpu.VMEM((4, 16, NX * COLS), F32),
            pltpu.VMEM((2, 16, NX * HALF), F32),
            pltpu.VMEM((6, 16, NX * HALF), BF16),
            pltpu.VMEM((6, 16, NX * HALF), BF16),
            pltpu.VMEM((16, NX * COLS), F32),
            pltpu.VMEM((16, NX * COLS), BF16),
            pltpu.VMEM((NX - 1, 16, COLS), BF16),
            dma((N_SENDS + 1,)),
            dma((N_GROUPS,)),
            dma((3,)),
        ],
        compiler_params=pltpu.CompilerParams(
            collective_id=0, has_side_effects=True, vmem_limit_bytes=58 << 20
        ),
        name="bucket_grads",
    )(tokens, upstream, weights)


def solution(mesh):
    placed = (
        P(("outer", "inner"), None),
        P(("outer", "inner"), None),
        P(None, ("outer", "inner"), None),
    )
    return jax.shard_map(
        on_device, mesh=mesh, in_specs=placed, out_specs=P(None, "inner", "outer"), check_vma=False
    )
```
